128 devices in a mesh: dom: 16 (over y, z), sub: 8 (over x, core).
Axes of the slice: x: 4, y: 4, z: 4, core: 2. Of those that a mesh axis runs over, the one named last changes fastest.
Arguments:
- nodes: bfloat16 [65536, 128], P(('dom', 'sub')), may hold values from -6 to 6
- edges: bfloat16 [262144, 128], P(('dom', 'sub')), may hold values from -6 to 6
- senders: int32 [262144], P(('dom', 'sub')), may hold values from 0 to 895
- receivers: int32 [262144], P(('dom', 'sub')), may hold values from 0 to 511
- edge_live: int32 [262144], P(('dom', 'sub')), may hold values from 0 to 1, as said below
- outlet_flags: int32 [65536], P(('dom', 'sub')), may hold values 0 or 1
- send_rows: int32 [49152], P(('dom', 'sub')), may hold values from 0 to 511
- edge_first: float32 [3, 384, 128], replicated, may hold values from -0.3125 to 0.3125
- edge_bias: float32 [3, 128], replicated, may hold values from -3 to 3
- edge_second: float32 [3, 128, 128], replicated, may hold values from -0.5 to 0.5
- edge_offset: float32 [3, 128], replicated, may hold values from -3 to 3
- edge_gain: float32 [3, 128], replicated, may hold values from 0.25 to 1.75
- node_first: float32 [3, 256, 128], replicated, may hold values from -0.375 to 0.375
- node_bias: float32 [3, 128], replicated, may hold values from -3 to 3
- node_second: float32 [3, 128, 128], replicated, may hold values from -0.5 to 0.5
- node_offset: float32 [3, 128], replicated, may hold values from -3 to 3
- node_gain: float32 [3, 128], replicated, may hold values from 0.25 to 1.75
- outlet_map: float32 [3, 128, 128], replicated, may hold values from -0.5 to 0.5
- grad_out: float32 [65536, 128], P(('dom', 'sub')), may hold values from -6 to 6
Outputs:
- latent_out: float32 [65536, 128], P(('dom', 'sub'))
- latent_grad: float32 [65536, 128], P(('dom', 'sub'))
- edge_first_grad: float32 [3, 384, 128], replicated
- edge_bias_grad: float32 [3, 128], replicated
- edge_second_grad: float32 [3, 128, 128], replicated
- edge_offset_grad: float32 [3, 128], replicated
- edge_gain_grad: float32 [3, 128], replicated
- node_first_grad: float32 [3, 256, 128], replicated
- node_bias_grad: float32 [3, 128], replicated
- node_second_grad: float32 [3, 128, 128], replicated
- node_offset_grad: float32 [3, 128], replicated
- node_gain_grad: float32 [3, 128], replicated
- outlet_map_grad: float32 [3, 128, 128], replicated
The draws below stay inside these ranges and needn't reach their ends.
Inputs may be any that keep to these rules, and one draw needn't show every extreme that they name: `edge_live`: on each device the live edge slots are the first ones of its 2048; each device has between a quarter and all of them live, and some device has all live. `senders`: indices below 512 name the device's own nodes; higher ones name halo rows.
All inputs are finite; a program needn't handle non-finite values. No bound on the sum of `outlet_flags` on one device may be relied on, other than what follows from the above.
Results may differ from the reference program's by a relative error of at most 0.018.
Values may be sent and summed in bfloat16 or wider, within the bound.
No kernel may reach another device: no remote copies, remote signals or barrier semaphores. Data moves between devices by JAX's collectives and lax.ppermute only.
A program may use at most 320 MiB of HBM per device.

```python
import jax
import jax.numpy as jnp
from jax import lax

D = 128
HID = 128
LAYERS = 3
NODE_DEV = 512
EDGE_DEV = 2048
SIDE_SUB = 64
SIDE_DOM = 128
SEND_DEV = 384
NODES = 65536
EDGES = 262144
N_DOM = 16
N_SUB = 8


def draw_edge_live(key, part):
    count_key, pick_key = jax.random.split(jax.random.fold_in(key, 17))
    devices = EDGES // EDGE_DEV
    counts = jax.random.randint(count_key, (devices,), EDGE_DEV // 4, EDGE_DEV + 1)
    chosen = jax.random.randint(pick_key, (), 0, devices)
    counts = jnp.where(jnp.arange(devices) == chosen, EDGE_DEV, counts)
    live = jnp.arange(EDGE_DEV)[None, :] < counts[:, None]
    return live.astype(jnp.int32).reshape(EDGES)


def set_ends(entries, rng, low, largest):
    longest = entries.shape.index(max(entries.shape))
    spots = []
    for shift in (0, 1):
        where = [jax.random.randint(jax.random.fold_in(rng, axis), (), 0, length) for axis, length in enumerate(entries.shape)]
        where[longest] = (where[longest] + shift) % entries.shape[longest]
        spots.append(tuple(where))
    return entries.at[spots[0]].set(low).at[spots[1]].set(largest)


def block_scale(own_key, shape, pieces, low, high):
    loudness, own = 1.0, jax.random.fold_in(own_key, 6)
    for dim, parts in pieces:
        steps = jnp.exp(jax.random.uniform(jax.random.fold_in(own, dim), (parts,), jnp.float32, low / len(pieces), high / len(pieces)))
        loudness = loudness * jnp.repeat(steps, shape[dim] // parts).reshape([-1 if axis == dim else 1 for axis in range(len(shape))])
    return loudness


def normal_values(stream_key, shape, scale, limit, cuts=(), dtype=jnp.bfloat16):
    result = scale * jax.random.normal(stream_key, shape, jnp.float32)
    if cuts:
        result = result * block_scale(stream_key, shape, cuts, -0.22, 0.18)
    return jnp.clip(result, -limit, limit).astype(dtype)


def setup_inputs(seed: int = 0) -> dict:
    arg_keys = jax.random.split(jax.random.key(seed), 20)
    return {
        "nodes": normal_values(arg_keys[0], (NODES, D), 1.0, 6.0, ((0, 128),)),
        "edges": normal_values(arg_keys[1], (EDGES, D), 1.0, 6.0, ((0, 128),)),
        "senders": set_ends(jax.random.randint(arg_keys[2], (EDGES,), 0, NODE_DEV + SEND_DEV), jax.random.fold_in(arg_keys[2], 1), 0, (NODE_DEV + SEND_DEV) - 1).astype(jnp.int32),
        "receivers": set_ends(jax.random.randint(arg_keys[3], (EDGES,), 0, NODE_DEV), jax.random.fold_in(arg_keys[3], 1), 0, NODE_DEV - 1).astype(jnp.int32),
        "edge_live": draw_edge_live(jax.random.fold_in(arg_keys[19], 71), 0),
        "outlet_flags": set_ends((jax.random.randint(arg_keys[5], (NODES,), 0, 8) < 1).astype(jnp.int32), jax.random.fold_in(arg_keys[5], 1), 0, 1),
        "send_rows": set_ends(jax.random.randint(arg_keys[6], (N_DOM * N_SUB * SEND_DEV,), 0, NODE_DEV), jax.random.fold_in(arg_keys[6], 1), 0, NODE_DEV - 1).astype(jnp.int32),
        "edge_first": normal_values(arg_keys[7], (LAYERS, 3 * D, HID), (3 * D) ** -0.5, 0.3125, (), jnp.float32),
        "edge_bias": normal_values(arg_keys[8], (LAYERS, HID), 0.5, 3.0, (), jnp.float32),
        "edge_second": normal_values(arg_keys[9], (LAYERS, HID, D), HID ** -0.5, 0.5, (), jnp.float32),
        "edge_offset": normal_values(arg_keys[10], (LAYERS, D), 0.5, 3.0, (), jnp.float32),
        "edge_gain": jnp.clip(1.0 + 0.15 * jax.random.normal(arg_keys[11], (LAYERS, D), jnp.float32), 0.25, 1.75),
        "node_first": normal_values(arg_keys[12], (LAYERS, 2 * D, HID), (2 * D) ** -0.5, 0.375, (), jnp.float32),
        "node_bias": normal_values(arg_keys[13], (LAYERS, HID), 0.5, 3.0, (), jnp.float32),
        "node_second": normal_values(arg_keys[14], (LAYERS, HID, D), HID ** -0.5, 0.5, (), jnp.float32),
        "node_offset": normal_values(arg_keys[15], (LAYERS, D), 0.5, 3.0, (), jnp.float32),
        "node_gain": jnp.clip(1.0 + 0.15 * jax.random.normal(arg_keys[16], (LAYERS, D), jnp.float32), 0.25, 1.75),
        "outlet_map": normal_values(arg_keys[17], (LAYERS, D, D), D ** -0.5, 0.5, (), jnp.float32),
        "grad_out": normal_values(arg_keys[18], (NODES, D), 1.0, 6.0, ((0, 128),), jnp.float32),
    }


def normalize(values):
    mean = lax.optimization_barrier(jnp.mean(values, axis=-1, keepdims=True))
    centered = values - mean
    variance = lax.optimization_barrier(jnp.mean(centered * centered, axis=-1, keepdims=True))
    return centered * lax.rsqrt(variance + 1e-05)

def layer_local(latent, edge_state, halo, layer_weights, senders, receivers, live, flags):
    edge_first, edge_bias, edge_second, edge_offset, edge_gain, node_first, node_bias, node_second, node_offset, node_gain, outlet_map = layer_weights
    own = latent.astype(jnp.bfloat16)
    extended = jnp.concatenate([own, halo], axis=0)
    joined = jnp.concatenate([edge_state.astype(jnp.bfloat16), extended[senders], own[receivers]], axis=1)
    act_one = jax.nn.silu(jnp.dot(joined, edge_first.astype(jnp.bfloat16), preferred_element_type=jnp.float32) + edge_bias).astype(jnp.bfloat16)
    pre_two = jnp.dot(act_one, edge_second.astype(jnp.bfloat16), preferred_element_type=jnp.float32) + edge_offset
    message = live[:, None] * (edge_gain * normalize(pre_two))
    new_edge = edge_state + message
    summed = jax.ops.segment_sum(message, receivers, num_segments=latent.shape[0])
    summed_half = summed.astype(jnp.bfloat16)
    node_in = jnp.concatenate([own, summed_half], axis=1)
    node_hidden = jax.nn.silu(jnp.dot(node_in, node_first.astype(jnp.bfloat16), preferred_element_type=jnp.float32) + node_bias).astype(jnp.bfloat16)
    update = node_gain * normalize(jnp.dot(node_hidden, node_second.astype(jnp.bfloat16), preferred_element_type=jnp.float32) + node_offset)
    outlet = flags[:, None] * jnp.dot(summed_half, outlet_map.astype(jnp.bfloat16), preferred_element_type=jnp.float32)
    return (latent + update + outlet, new_edge)

def exchange_rows(latent, send):
    count = N_DOM * N_SUB
    low = SIDE_SUB
    high = SIDE_DOM
    sent = jax.vmap(lambda rows, picks: rows[picks])(latent, send).astype(jnp.bfloat16)
    grid = sent.reshape(N_DOM, N_SUB, SEND_DEV, D)
    zero_sub = jnp.zeros((N_DOM, 1, low, D), jnp.bfloat16)
    zero_dom = jnp.zeros((1, N_SUB, high, D), jnp.bfloat16)
    from_lower = jnp.concatenate([zero_sub, grid[:, :-1, low:2 * low]], axis=1)
    from_upper = jnp.concatenate([grid[:, 1:, :low], zero_sub], axis=1)
    dom_lower = jnp.concatenate([zero_dom, grid[:-1, :, 2 * low + high:]], axis=0)
    dom_upper = jnp.concatenate([grid[1:, :, 2 * low:2 * low + high], zero_dom], axis=0)
    halo = jnp.concatenate([from_lower, from_upper, dom_lower, dom_upper], axis=2)
    return halo.reshape(count, SEND_DEV, D)

def reference(nodes, edges, senders, receivers, edge_live, outlet_flags, send_rows, edge_first, edge_bias, edge_second, edge_offset, edge_gain, node_first, node_bias, node_second, node_offset, node_gain, outlet_map, grad_out):
    count = N_DOM * N_SUB
    latent_start = nodes.astype(jnp.float32).reshape(count, NODE_DEV, D)
    edge_start = edges.astype(jnp.float32).reshape(count, EDGE_DEV, D)
    send = send_rows.reshape(count, SEND_DEV)
    sender_idx = senders.reshape(count, EDGE_DEV)
    receiver_idx = receivers.reshape(count, EDGE_DEV)
    live = edge_live.astype(jnp.float32).reshape(count, EDGE_DEV)
    flags = outlet_flags.astype(jnp.float32).reshape(count, NODE_DEV)
    weights = (edge_first, edge_bias, edge_second, edge_offset, edge_gain, node_first, node_bias, node_second, node_offset, node_gain, outlet_map)
    copies = tuple((jnp.broadcast_to(weight[None], (count,) + weight.shape) for weight in weights))

    def one_layer(latent, edge_state, layer_copies):
        halo = exchange_rows(latent, send)
        return jax.vmap(layer_local)(latent, edge_state, halo, layer_copies, sender_idx, receiver_idx, live, flags)
    checked = jax.checkpoint(one_layer)

    def forward(latent, all_copies):
        edge_state = edge_start
        for layer in range(LAYERS):
            latent, edge_state = checked(latent, edge_state, tuple((copy[:, layer] for copy in all_copies)))
        return latent
    final, pullback = jax.vjp(forward, latent_start, copies)
    latent_grad, copy_grads = pullback(grad_out.reshape(count, NODE_DEV, D))
    summed = tuple((lax.optimization_barrier(jnp.sum(grad, axis=0)) for grad in copy_grads))
    g_ef, g_eb, g_es, g_eo, g_eg, g_nf, g_nb, g_ns, g_no, g_ng, g_om = summed
    return (final.reshape(NODES, D), latent_grad.reshape(NODES, D), g_ef, g_eb, g_es, g_eo, g_eg, g_nf, g_nb, g_ns, g_no, g_ng, g_om)
```

```python
import types

import jax
import jax.numpy as jnp
from jax import lax
from jax.experimental import pallas as pl
from jax.experimental.pallas import tpu as pltpu
from jax.sharding import PartitionSpec as P

BF = jnp.bfloat16
F32 = jnp.float32
I32 = jnp.int32
D = 128
AXES = ("dom", "sub")
CHUNK = 512

MATRICES = ("edge_first", "edge_second", "node_first", "node_second", "outlet_map")
VECTORS = ("edge_bias", "edge_offset", "edge_gain", "node_bias", "node_offset", "node_gain")


def dot(a, b):
    return jnp.dot(a, b, preferred_element_type=F32)


def dot_nt(a, b):
    return lax.dot_general(a, b, (((1,), (1,)), ((), ())), preferred_element_type=F32)


def dot_tn(a, b):
    return lax.dot_general(a, b, (((0,), (0,)), ((), ())), preferred_element_type=F32)


def sigmoid(x):
    return 0.5 * jnp.tanh(0.5 * x) + 0.5


def layer_norm(v):
    centered = v - jnp.mean(v, axis=-1, keepdims=True)
    inverse = lax.rsqrt(jnp.mean(centered * centered, axis=-1, keepdims=True) + 1e-05)
    return centered * inverse, inverse


def layer_norm_back(grad, normal, inverse):
    mean = jnp.mean(grad, axis=-1, keepdims=True)
    along = jnp.mean(grad * normal, axis=-1, keepdims=True)
    return inverse * (grad - mean - normal * along)


def one_hot_columns(index, count):
    lane = lax.broadcasted_iota(I32, index.shape, 1).astype(F32)
    parts = [jnp.where(index == lane + float(D * k), 1.0, 0.0).astype(BF) for k in range(count)]
    return parts[0] if count == 1 else jnp.concatenate(parts, axis=1)


def one_hot_rows(rows, count):
    place = lax.broadcasted_iota(I32, (count, D), 0)
    parts = [jnp.where(place == row, 1.0, 0.0).astype(BF) for row in rows]
    return parts[0] if len(parts) == 1 else jnp.concatenate(parts, axis=1)


def column(row):
    corner = lax.broadcasted_iota(I32, (D, D), 0) == lax.broadcasted_iota(I32, (D, D), 1)
    total = jnp.sum(jnp.where(corner, jnp.broadcast_to(row, (D, D)), 0.0), axis=1, keepdims=True)
    return jnp.broadcast_to(total, (D, D))


def fill_columns(target, values):
    for k in range(values.shape[0]):
        target[D * k : D * (k + 1), :] = column(values[k : k + 1, :])


def run(body, ins, outs, scratch=(), flops=0):
    names = [name for name, _ in ins] + [name for name, _, _ in outs] + [name for name, _, _ in scratch]

    def kernel(*refs):
        body(types.SimpleNamespace(**dict(zip(names, refs))))

    vmem = pltpu.VMEM
    smem = pltpu.SMEM
    results = pl.pallas_call(
        kernel,
        out_shape=[jax.ShapeDtypeStruct(shape, dtype) for _, shape, dtype in outs],
        in_specs=[pl.BlockSpec(memory_space=smem if name == "parity" else vmem) for name, _ in ins],
        out_specs=[pl.BlockSpec(memory_space=vmem) for _ in outs],
        scratch_shapes=[pltpu.VMEM(shape, dtype) for _, shape, dtype in scratch],
        compiler_params=pltpu.CompilerParams(vmem_limit_bytes=40 << 20),
        cost_estimate=pl.CostEstimate(flops=flops, bytes_accessed=4 << 20, transcendentals=0),
    )(*[value for _, value in ins])
    return dict(zip([name for name, _, _ in outs], results))


def write_sent(r, own, rows):
    columns = [column(row.astype(F32)) for row in rows]
    picks = one_hot_columns(jnp.concatenate(columns, axis=0), 4)
    sent = dot(picks, own).astype(BF)
    r.sent0[...] = sent[0:64]
    r.sent1[...] = sent[64:128]
    r.sent2[...] = sent[128:256]
    r.sent3[...] = sent[256:384]


SENT = [("sent0", (64, D), BF), ("sent1", (64, D), BF), ("sent2", (128, D), BF), ("sent3", (128, D), BF)]


def start_body(r):
    sub_even = r.parity[0] == 1
    dom_even = r.parity[1] == 1
    row0 = r.send_rows[0:1, :]
    row1 = r.send_rows[1:2, :]
    row2 = r.send_rows[2:3, :]
    turned = jnp.concatenate([row0[:, 64:], row0[:, :64]], axis=1)
    first = jnp.where(sub_even, turned, row0)
    second = jnp.where(dom_even, row2, row1)
    third = jnp.where(dom_even, row1, row2)
    r.send_out[0:1, :] = first
    r.send_out[1:2, :] = second
    r.send_out[2:3, :] = third
    senders = r.senders[...]
    halo = senders - 512
    near = jnp.bitwise_xor(halo, jnp.where(sub_even, 64, 0)) + 512
    far = jnp.bitwise_xor(halo - 128, jnp.where(dom_even, 128, 0)) + 640
    r.senders_out[...] = jnp.where(halo < 0, senders, jnp.where(halo < 128, near, far))
    write_sent(r, r.nodes[...], (first, second, third))


def gather_setup(r, own):
    r.ext2[:, 0:128] = own
    r.ext2[0:64, 128:256] = r.halo0[...]
    r.ext2[64:128, 128:256] = r.halo1[...]
    r.ext2[128:256, 128:256] = r.halo2[...]
    r.ext2[256:384, 128:256] = r.halo3[...]
    r.ext2[384:512, 128:256] = jnp.zeros((128, 128), BF)


def forward_part(r, layer, z1, pre2, zn, pn, half, keep_edges, send):
    own = r.latent[...].astype(BF)
    gather_setup(r, own)
    r.own2[:, 0:128] = own[0:256]
    r.own2[:, 128:256] = own[256:512]
    w1 = r.edge_first[layer].astype(BF)
    w2 = r.edge_second[layer].astype(BF)
    b1 = r.edge_bias[layer : layer + 1, :]
    b2 = r.edge_offset[layer : layer + 1, :]
    gain = r.edge_gain[layer : layer + 1, :]
    r.total[...] = jnp.zeros(r.total.shape, F32)

    def chunk(c, carry):
        rows = pl.ds(pl.multiple_of(c * CHUNK, CHUNK), CHUNK)
        sender = r.col_send[rows, :]
        halo = sender >= 512.0
        picked = dot(one_hot_columns(jnp.where(halo, sender - 512.0, sender), 4), r.ext2[...])
        from_sender = jnp.where(halo, picked[:, 128:], picked[:, :128]).astype(BF)
        code = r.col_code[rows, :]
        receiver = jnp.where(halo, code - 512.0, code)
        upper = receiver >= 256.0
        picked = dot(one_hot_columns(jnp.where(upper, receiver - 256.0, receiver), 2), r.own2[...])
        at_receiver = jnp.where(upper, picked[:, 128:], picked[:, :128]).astype(BF)
        edge = r.edge[rows, :].astype(F32)
        joined = jnp.concatenate([edge.astype(BF), from_sender, at_receiver], axis=1)
        pre1 = dot(joined, w1) + b1
        z1[rows, :] = pre1
        act = (pre1 * sigmoid(pre1)).astype(BF)
        second = dot(act, w2) + b2
        pre2[rows, :] = second
        normal, _ = layer_norm(second)
        message = r.col_live[rows, :] * gain * normal
        if keep_edges:
            r.edge_out[rows, :] = edge + message
        top = message.astype(BF)
        rest = (message - top.astype(F32)).astype(BF)
        where = [r.receivers[pl.ds(c * (CHUNK // D) + k, 1), :] for k in range(CHUNK // D)]
        r.total[...] += dot(one_hot_rows(where, 512), jnp.concatenate([top, rest], axis=1))
        return carry

    lax.fori_loop(0, 2048 // CHUNK, chunk, 0)
    summed = (r.total[:, 0:128] + r.total[:, 128:256]).astype(BF)
    half[...] = summed
    hidden_in = dot(jnp.concatenate([own, summed], axis=1), r.node_first[layer].astype(BF))
    hidden_in = hidden_in + r.node_bias[layer : layer + 1, :]
    zn[...] = hidden_in
    hidden = (hidden_in * sigmoid(hidden_in)).astype(BF)
    last = dot(hidden, r.node_second[layer].astype(BF)) + r.node_offset[layer : layer + 1, :]
    pn[...] = last
    normal, _ = layer_norm(last)
    outlet = r.col_flag[...] * dot(summed, r.outlet_map[layer].astype(BF))
    latent = r.latent[...].astype(F32) + r.node_gain[layer : layer + 1, :] * normal + outlet
    r.latent_out[...] = latent
    if send:
        write_sent(r, latent.astype(BF), [r.send_rows[k : k + 1, :] for k in range(3)])


def returned_sum(r):
    spread = one_hot_rows([r.send_rows[k : k + 1, :] for k in range(3)], 512)
    back = jnp.concatenate([r.back0[...], r.back1[...], r.back2[...], r.back3[...]], axis=0)
    return dot(spread, back)


def backward_part(r, layer, grad, z1, pre2, zn, pn, half, has_edge_grad, keep_edge_grad):
    own = r.latent[...].astype(BF)
    n1 = r.node_first[layer].astype(BF)
    n2 = r.node_second[layer].astype(BF)
    om = r.outlet_map[layer].astype(BF)
    summed = half[...]
    hidden_in = zn[...]
    gate = sigmoid(hidden_in)
    hidden = (hidden_in * gate).astype(BF)
    normal, inverse = layer_norm(pn[...])
    r.vec[5:6, :] = jnp.sum(grad * normal, axis=0, keepdims=True)
    d_last = layer_norm_back(grad * r.node_gain[layer : layer + 1, :], normal, inverse)
    r.vec[4:5, :] = jnp.sum(d_last, axis=0, keepdims=True)
    d_last = d_last.astype(BF)
    d_hidden = dot_nt(d_last, n2).astype(BF).astype(F32)
    d_in = d_hidden * (gate * (1.0 + hidden_in * (1.0 - gate)))
    r.vec[3:4, :] = jnp.sum(d_in, axis=0, keepdims=True)
    d_in = d_in.astype(BF)
    d_node_in = dot_nt(d_in, n1)
    d_outlet = (grad * r.col_flag[...]).astype(BF)
    d_summed = (d_node_in[:, 128:] + dot_nt(d_outlet, om)).astype(BF)
    r.own2[:, 0:128] = d_summed[0:256]
    r.own2[:, 128:256] = d_summed[256:512]

    def put(start, value):
        count = value.shape[0] // 8
        r.weights_out[start : start + count] = value.reshape(count, 8, D).astype(r.weights_out.dtype)

    put(64, dot_tn(jnp.concatenate([own, summed], axis=1), d_in))
    put(96, dot_tn(hidden, d_last))
    put(112, dot_tn(summed, d_outlet))

    w1 = r.edge_first[layer].astype(BF)
    w2 = r.edge_second[layer].astype(BF)
    gain = r.edge_gain[layer : layer + 1, :]
    zero = jnp.zeros((1, D), F32)
    r.to_send[...] = jnp.zeros(r.to_send.shape, F32)
    r.to_recv[...] = jnp.zeros(r.to_recv.shape, F32)
    r.d_w2[...] = jnp.zeros((D, D), F32)
    r.d_w1[...] = jnp.zeros((D, D), F32)

    def chunk(c, carry):
        d_bias, d_offset, d_gain = carry
        rows = pl.ds(pl.multiple_of(c * CHUNK, CHUNK), CHUNK)
        code = r.col_code[rows, :]
        halo = code >= 512.0
        receiver = jnp.where(halo, code - 512.0, code)
        upper = receiver >= 256.0
        picked = dot(one_hot_columns(jnp.where(upper, receiver - 256.0, receiver), 2), r.own2[...])
        d_message = jnp.where(upper, picked[:, 128:], picked[:, :128])
        if has_edge_grad:
            d_message = d_message + r.edge_grad[rows, :]
        live = d_message * r.col_live[rows, :]
        normal, inverse = layer_norm(pre2[rows, :])
        d_gain = d_gain + jnp.sum(live * normal, axis=0, keepdims=True)
        d_second = layer_norm_back(live * gain, normal, inverse)
        d_offset = d_offset + jnp.sum(d_second, axis=0, keepdims=True)
        d_second = d_second.astype(BF)
        pre1 = z1[rows, :]
        gate = sigmoid(pre1)
        act = (pre1 * gate).astype(BF)
        d_act = dot_nt(d_second, w2).astype(BF).astype(F32)
        d_first = d_act * (gate * (1.0 + pre1 * (1.0 - gate)))
        d_bias = d_bias + jnp.sum(d_first, axis=0, keepdims=True)
        d_half = d_first.astype(BF)
        edge = r.edge[rows, :].astype(BF)
        r.d_w2[...] += dot_tn(act, d_second)
        r.d_w1[...] += dot_tn(edge, d_half)
        if keep_edge_grad:
            d_edge = dot_nt(d_half, w1[0:128]).astype(BF).astype(F32)
            r.edge_grad_out[rows, :] = d_edge + r.edge_grad[rows, :] if has_edge_grad else d_edge
        none = jnp.zeros((CHUNK, D), F32)
        split = jnp.concatenate([jnp.where(halo, none, d_first), jnp.where(halo, d_first, none)], axis=1)
        places = [r.senders[pl.ds(c * (CHUNK // D) + k, 1), :] for k in range(CHUNK // D)]
        places = [jnp.bitwise_and(place, 511) for place in places]
        r.to_send[...] += dot(one_hot_rows(places, 512), split.astype(BF))
        split = jnp.concatenate([jnp.where(upper, none, d_first), jnp.where(upper, d_first, none)], axis=1)
        places = [r.receivers[pl.ds(c * (CHUNK // D) + k, 1), :] for k in range(CHUNK // D)]
        places = [jnp.bitwise_and(place, 255) for place in places]
        r.to_recv[...] += dot(one_hot_rows(places, 256), split.astype(BF))
        return d_bias, d_offset, d_gain

    d_bias, d_offset, d_gain = lax.fori_loop(0, 2048 // CHUNK, chunk, (zero, zero, zero))
    r.vec[0:1, :] = d_bias
    r.vec[1:2, :] = d_offset
    r.vec[2:3, :] = d_gain
    r.vec[6:8, :] = jnp.zeros((2, D), F32)
    from_own = r.to_send[:, 0:128].astype(BF)
    from_halo = r.to_send[0:384, 128:256].astype(BF)
    at_recv = jnp.concatenate([r.to_recv[:, 0:128], r.to_recv[:, 128:256]], axis=0).astype(BF)
    d_halo = dot_nt(from_halo, w1[128:256]).astype(BF)
    r.sent0[...] = d_halo[0:64]
    r.sent1[...] = d_halo[64:128]
    r.sent2[...] = d_halo[128:256]
    r.sent3[...] = d_halo[256:384]
    r.grad_out[...] = grad + d_node_in[:, 0:128] + dot_nt(from_own, w1[128:256]) + dot_nt(at_recv, w1[256:384])
    halo = jnp.concatenate([r.halo0[...], r.halo1[...], r.halo2[...], r.halo3[...]], axis=0)
    put(0, r.d_w1[...])
    put(16, dot_tn(own, from_own) + dot_tn(halo, from_halo))
    put(32, dot_tn(own, at_recv))
    put(48, r.d_w2[...])


def fill_flag(r):
    fill_columns(r.col_flag, r.flags[...].astype(F32))


def fill_code(r):
    halo = jnp.where(r.senders[...] >= 512, 512, 0)
    fill_columns(r.col_code, (r.receivers[...] + halo).astype(F32))
    fill_columns(r.col_live, r.live[...].astype(F32))


def fill_send(r):
    fill_columns(r.col_send, r.senders[...].astype(F32))


EDGE_COLUMNS = [("col_code", (2048, D), F32), ("col_live", (2048, D), F32), ("col_flag", (512, D), F32)]
FORWARD_SCRATCH = [
    ("col_send", (2048, D), F32),
    ("ext2", (512, 256), BF),
    ("total", (512, 256), F32),
]
PAIR_SCRATCH = [("own2", (256, 256), BF)]
BACKWARD_SCRATCH = [
    ("to_send", (512, 256), F32),
    ("to_recv", (256, 256), F32),
    ("d_w1", (D, D), F32),
    ("d_w2", (D, D), F32),
]
RESIDUALS = [
    ("z1", (2048, D), F32),
    ("pre2", (2048, D), F32),
    ("zn", (512, D), F32),
    ("pn", (512, D), F32),
    ("half", (512, D), BF),
]


def pairs(axis, odd):
    count = lax.axis_size(axis)
    steps = []
    for low in range(odd, count - 1, 2):
        steps += [(low, low + 1), (low + 1, low)]
    return steps


def exchange(made, names):
    moved = []
    for k, (axis, odd) in enumerate((("sub", 0), ("sub", 1), ("dom", 0), ("dom", 1))):
        moved.append(lax.ppermute(made["sent%d" % k], axis, pairs(axis, odd)))
    return [(names + str(k), moved[k]) for k in range(4)]


def on_device(nodes, edges, senders, receivers, edge_live, outlet_flags, send_rows, *rest):
    weights = dict(
        zip(
            (
                "edge_first",
                "edge_bias",
                "edge_second",
                "edge_offset",
                "edge_gain",
                "node_first",
                "node_bias",
                "node_second",
                "node_offset",
                "node_gain",
                "outlet_map",
            ),
            rest[:-1],
        )
    )
    grad_out = rest[-1]
    weight_ins = list(weights.items())
    parity = jnp.stack([1 - lax.axis_index("sub") % 2, 1 - lax.axis_index("dom") % 2]).astype(I32)
    receivers = receivers.reshape(16, D)
    shared = [
        ("receivers", receivers),
        ("live", edge_live.reshape(16, D)),
        ("flags", outlet_flags.reshape(4, D)),
    ]
    first = run(
        start_body,
        [("parity", parity), ("nodes", nodes), ("senders", senders.reshape(16, D)), ("send_rows", send_rows.reshape(3, D))],
        SENT + [("send_out", (3, D), I32), ("senders_out", (16, D), I32)],
    )
    shared += [("senders", first["senders_out"]), ("send_rows", first["send_out"])]
    made = first
    latent, edge = nodes, edges
    entered = []
    for layer in range(2):
        halo = exchange(made, "halo")

        def forward(r, layer=layer):
            fill_flag(r)
            fill_code(r)
            fill_send(r)
            forward_part(r, layer, r.z1, r.pre2, r.zn, r.pn, r.half, True, True)

        ins = shared + halo + [("latent", latent), ("edge", edge)] + weight_ins
        made = run(
            forward,
            ins,
            SENT + [("latent_out", (512, D), F32), ("edge_out", (2048, D), F32)] + RESIDUALS,
            EDGE_COLUMNS + FORWARD_SCRATCH + PAIR_SCRATCH,
            flops=4 << 30,
        )
        entered.append((ins, made))
        latent, edge = made["latent_out"], made["edge_out"]

    halo = exchange(made, "halo")

    def turn(r):
        fill_flag(r)
        fill_code(r)
        fill_send(r)
        forward_part(r, 2, r.z1, r.pre2, r.zn, r.pn, r.half, False, False)
        backward_part(r, 2, r.top_grad[...], r.z1, r.pre2, r.zn, r.pn, r.half, False, True)

    gradient_outs = SENT + [("grad_out", (512, D), F32), ("vec", (8, D), F32)]
    made = run(
        turn,
        shared + halo + [("latent", latent), ("edge", edge), ("top_grad", grad_out)] + weight_ins,
        gradient_outs
        + [("weights_out", (128, 8, D), BF), ("latent_out", (512, D), F32), ("edge_grad_out", (2048, D), F32)],
        EDGE_COLUMNS + FORWARD_SCRATCH + PAIR_SCRATCH + BACKWARD_SCRATCH + RESIDUALS,
        flops=12 << 30,
    )
    latent_out = made["latent_out"]
    collected = [None, None, (made["weights_out"], made["vec"])]
    for layer in (1, 0):
        back = exchange(made, "back")
        ins, held = entered[layer]

        def backward(r, layer=layer):
            fill_flag(r)
            fill_code(r)
            grad = r.top_grad[...] + returned_sum(r)
            backward_part(r, layer, grad, r.z1, r.pre2, r.zn, r.pn, r.half, True, layer > 0)

        residuals = [(name, held[name]) for name, _, _ in RESIDUALS]
        made = run(
            backward,
            ins + back + residuals + [("top_grad", made["grad_out"]), ("edge_grad", made["edge_grad_out"])],
            gradient_outs
            + [("weights_out", (128, 8, D), BF)]
            + ([("edge_grad_out", (2048, D), F32)] if layer else []),
            EDGE_COLUMNS + PAIR_SCRATCH + BACKWARD_SCRATCH,
            flops=8 << 30,
        )
        collected[layer] = (made["weights_out"], made["vec"])

    def pack(r):
        for layer in range(3):
            r.packed[:, 8 * layer : 8 * layer + 8, :] = getattr(r, "weights%d" % layer)[...]
        vec = jnp.concatenate([r.vec0[...], r.vec1[...], r.vec2[...]], axis=0)
        top = vec.astype(BF).astype(F32)
        rest = (vec - top).astype(BF).astype(F32)
        tall = jnp.concatenate([top, rest, jnp.zeros((80, D), F32)], axis=0)
        turned = jnp.transpose(tall)
        r.packed[:, 24:32, :] = jnp.broadcast_to(turned.reshape(128, 1, D), (128, 8, D)).astype(BF)

    back = exchange(made, "back")
    packed = run(
        pack,
        [("weights%d" % k, collected[k][0]) for k in range(3)] + [("vec%d" % k, collected[k][1]) for k in range(3)],
        [("packed", (128, 32, D), BF)],
    )["packed"]
    shares = lax.all_to_all(packed, AXES, 0, 0, tiled=True)

    def middle(r):
        r.latent_grad[...] = r.top_grad[...] + returned_sum(r)
        r.summed[...] = jnp.sum(r.shares[...].astype(F32), axis=0)

    mid = run(
        middle,
        [("send_rows", first["send_out"]), ("top_grad", made["grad_out"]), ("shares", shares)] + back,
        [("latent_grad", (512, D), F32), ("summed", (32, D), F32)],
    )
    spread = jnp.broadcast_to(mid["summed"][None], (128, 32, D))
    whole = lax.all_to_all(spread, AXES, 0, 0, tiled=True)

    def finish(r):
        for layer in range(3):
            start = 0
            for name in MATRICES:
                rows = weights[name].shape[1]
                block = r.whole[start : start + rows // 8, 8 * layer : 8 * layer + 8, :]
                getattr(r, name)[layer] = block.reshape(rows, D)
                start += rows // 8
        turned = jnp.transpose(r.whole[:, 24, :])
        vec = turned[0:24] + turned[24:48]
        for layer in range(3):
            for k, name in enumerate(VECTORS):
                getattr(r, name)[layer : layer + 1, :] = vec[8 * layer + k : 8 * layer + k + 1, :]

    results = run(finish, [("whole", whole)], [(name, value.shape, F32) for name, value in weight_ins])
    return (latent_out, mid["latent_grad"]) + tuple(results[name] for name, _ in weight_ins)


def solution(mesh):
    split = P(AXES, None)
    flat = P(AXES)
    placed = (split, split) + (flat,) * 5 + (P(),) * 11 + (split,)
    return jax.shard_map(
        on_device,
        mesh=mesh,
        in_specs=placed,
        out_specs=(split, split) + (P(),) * 11,
        check_vma=False,
    )
```

```python
import types

import jax
import jax.numpy as jnp
from jax import lax
from jax.experimental import pallas as pl
from jax.experimental.pallas import tpu as pltpu
from jax.sharding import PartitionSpec as P

BF = jnp.bfloat16
F32 = jnp.float32
I32 = jnp.int32
D = 128
AXES = ("dom", "sub")
CHUNK = 512
VMEM_LIMIT = 20 << 20

MATRICES = ("edge_first", "edge_second", "node_first", "node_second", "outlet_map")
VECTORS = ("edge_bias", "edge_offset", "edge_gain", "node_bias", "node_offset", "node_gain")


def dot(a, b):
    return jnp.dot(a, b, preferred_element_type=F32)


def dot_nt(a, b):
    return lax.dot_general(a, b, (((1,), (1,)), ((), ())), preferred_element_type=F32)


def dot_tn(a, b):
    return lax.dot_general(a, b, (((0,), (0,)), ((), ())), preferred_element_type=F32)


def sigmoid(x):
    return 0.5 * jnp.tanh(0.5 * x) + 0.5


def layer_norm(v):
    centered = v - jnp.mean(v, axis=-1, keepdims=True)
    inverse = lax.rsqrt(jnp.mean(centered * centered, axis=-1, keepdims=True) + 1e-05)
    return centered * inverse, inverse


def layer_norm_back(grad, normal, inverse):
    mean = jnp.mean(grad, axis=-1, keepdims=True)
    along = jnp.mean(grad * normal, axis=-1, keepdims=True)
    return inverse * (grad - mean - normal * along)


def one_hot_columns(index, count):
    lane = lax.broadcasted_iota(I32, index.shape, 1).astype(F32)
    parts = [jnp.where(index == lane + float(D * k), 1.0, 0.0).astype(BF) for k in range(count)]
    return parts[0] if count == 1 else jnp.concatenate(parts, axis=1)


def one_hot_rows(rows, count):
    place = lax.broadcasted_iota(I32, (count, D), 0)
    parts = [jnp.where(place == row, 1.0, 0.0).astype(BF) for row in rows]
    return parts[0] if len(parts) == 1 else jnp.concatenate(parts, axis=1)


def column(row):
    corner = lax.broadcasted_iota(I32, (D, D), 0) == lax.broadcasted_iota(I32, (D, D), 1)
    total = jnp.sum(jnp.where(corner, jnp.broadcast_to(row, (D, D)), 0.0), axis=1, keepdims=True)
    return jnp.broadcast_to(total, (D, D))


def fill_columns(target, values):
    for k in range(values.shape[0]):
        target[D * k : D * (k + 1), :] = column(values[k : k + 1, :])


def run(body, ins, outs, scratch=(), flops=0, held=()):
    names = [name for name, _ in ins] + [name for name, _, _ in outs] + [name for name, _, _ in scratch]

    def kernel(*refs):
        body(types.SimpleNamespace(**dict(zip(names, refs))))

    results = pl.pallas_call(
        kernel,
        out_shape=[jax.ShapeDtypeStruct(shape, dtype) for _, shape, dtype in outs],
        in_specs=[pl.BlockSpec(memory_space=pltpu.HBM if name in held else pltpu.VMEM) for name, _ in ins],
        out_specs=[pl.BlockSpec(memory_space=pltpu.VMEM) for _ in outs],
        scratch_shapes=[
            pltpu.SemaphoreType.DMA(shape) if dtype is None else pltpu.VMEM(shape, dtype)
            for _, shape, dtype in scratch
        ],
        compiler_params=pltpu.CompilerParams(vmem_limit_bytes=VMEM_LIMIT),
        cost_estimate=pl.CostEstimate(flops=flops, bytes_accessed=4 << 20, transcendentals=0),
    )(*[pltpu.with_memory_space_constraint(value, pltpu.HBM) if name in held else value for name, value in ins])
    return dict(zip([name for name, _, _ in outs], results))


def fetch(r, moves):
    copies = [pltpu.make_async_copy(source, target, r.sem.at[k]) for k, (source, target) in enumerate(moves)]
    for copy in copies:
        copy.start()
    for copy in copies:
        copy.wait()


def write_sent(r, own, rows):
    columns = [column(row.astype(F32)) for row in rows]
    picks = one_hot_columns(jnp.concatenate(columns, axis=0), 4)
    sent = dot(picks, own).astype(BF)
    r.sent0[...] = sent[0:64]
    r.sent1[...] = sent[64:128]
    r.sent2[...] = sent[128:256]
    r.sent3[...] = sent[256:384]


def even(axis):
    return lax.rem(lax.axis_index(axis), 2) == 0


def start_body(r):
    fetch(r, [(r.nodes_in, r.nodes), (r.rows_in, r.rows)])
    sub_even, dom_even = even("sub"), even("dom")
    row0, row1, row2 = (r.rows[k : k + 1, :] for k in range(3))
    turned = jnp.concatenate([row0[:, 64:], row0[:, :64]], axis=1)
    first = jnp.where(sub_even, turned, row0)
    second = jnp.where(dom_even, row2, row1)
    third = jnp.where(dom_even, row1, row2)
    r.send_rows[0:1, :] = first
    r.send_rows[1:2, :] = second
    r.send_rows[2:3, :] = third
    write_sent(r, r.nodes[...], (first, second, third))


def load_body(r):
    moves = [(getattr(r, name + "_in"), getattr(r, name)) for name in COPIED]
    moves += [(getattr(r, name), getattr(r, name + "_raw")) for name in MATRICES + VECTORS]
    fetch(r, moves)
    sub_even, dom_even = even("sub"), even("dom")
    senders = r.senders[...]
    halo = senders - 512
    near = jnp.bitwise_xor(halo, jnp.where(sub_even, 64, 0)) + 512
    far = jnp.bitwise_xor(halo - 128, jnp.where(dom_even, 128, 0)) + 640
    senders = jnp.where(halo < 0, senders, jnp.where(halo < 128, near, far))
    receivers = r.receivers[...]
    outside = senders >= 512
    places = jnp.bitwise_and(senders, 511)
    for k in range(16):
        rows = slice(D * k, D * (k + 1))
        place = places[k : k + 1, :]
        receiver = receivers[k : k + 1, :]
        r.hot_send_t[:, rows] = one_hot_rows([place], 512)
        wide = one_hot_rows([receiver], 512)
        r.hot_recv_t[:, rows] = wide
        r.hot_half_t[:, rows] = wide[0:256] + wide[256:512]
        r.hot_send[rows, :] = one_hot_columns(column(place.astype(F32)), 4)
        at = column(receiver.astype(F32))
        upper = jnp.where(at >= 256.0, 1.0, 0.0)
        r.hot_recv[rows, :] = one_hot_columns(at - 256.0 * upper, 2)
        r.upper[rows, :] = upper
        r.outside[rows, :] = column(jnp.where(outside[k : k + 1, :], 1.0, 0.0))
        r.alive[rows, :] = column(r.live[k : k + 1, :].astype(F32))
    fill_columns(r.flag, r.flags[...].astype(F32))
    for layer in range(3):
        start = 0
        for name in MATRICES:
            value = getattr(r, name + "_raw")[layer].astype(BF)
            r.weights[layer, start : start + value.shape[0], :] = value
            start += value.shape[0]
        for k, name in enumerate(VECTORS):
            r.vectors[layer, k : k + 1, :] = getattr(r, name + "_raw")[layer : layer + 1, :]


def gather_setup(r, own):
    r.ext2[:, 0:128] = own
    r.ext2[0:64, 128:256] = r.halo0[...]
    r.ext2[64:128, 128:256] = r.halo1[...]
    r.ext2[128:256, 128:256] = r.halo2[...]
    r.ext2[256:384, 128:256] = r.halo3[...]
    r.ext2[384:512, 128:256] = jnp.zeros((128, 128), BF)


def matrix(r, layer, name):
    first, count = PLACES[name]
    return r.weights[layer, first : first + count, :]


def vector(r, layer, name):
    k = VECTORS.index(name)
    return r.vectors[layer, k : k + 1, :]


def forward_part(r, layer, keep_edges, send):
    own = r.latent[...].astype(BF)
    gather_setup(r, own)
    r.own2[:, 0:128] = own[0:256]
    r.own2[:, 128:256] = own[256:512]
    w1 = matrix(r, layer, "edge_first")
    w2 = matrix(r, layer, "edge_second")
    b1 = vector(r, layer, "edge_bias")
    b2 = vector(r, layer, "edge_offset")
    gain = vector(r, layer, "edge_gain")
    r.total[...] = jnp.zeros(r.total.shape, F32)

    def chunk(c, carry):
        rows = pl.ds(pl.multiple_of(c * CHUNK, CHUNK), CHUNK)
        picked = dot(r.hot_send[rows, :], r.ext2[...])
        from_sender = jnp.where(r.outside[rows, :] > 0.5, picked[:, 128:], picked[:, :128]).astype(BF)
        picked = dot(r.hot_recv[rows, :], r.own2[...])
        at_receiver = jnp.where(r.upper[rows, :] > 0.5, picked[:, 128:], picked[:, :128]).astype(BF)
        edge = r.edge[rows, :].astype(F32)
        joined = jnp.concatenate([edge.astype(BF), from_sender, at_receiver], axis=1)
        pre1 = dot(joined, w1) + b1
        r.z1[rows, :] = pre1
        act = (pre1 * sigmoid(pre1)).astype(BF)
        second = dot(act, w2) + b2
        r.pre2[rows, :] = second
        normal, _ = layer_norm(second)
        message = r.alive[rows, :] * gain * normal
        if keep_edges:
            r.edge_out[rows, :] = edge + message
        top = message.astype(BF)
        rest = (message - top.astype(F32)).astype(BF)
        r.total[...] += dot(r.hot_recv_t[:, rows], jnp.concatenate([top, rest], axis=1))
        return carry

    lax.fori_loop(0, 2048 // CHUNK, chunk, 0)
    summed = (r.total[:, 0:128] + r.total[:, 128:256]).astype(BF)
    r.half[...] = summed
    hidden_in = dot(jnp.concatenate([own, summed], axis=1), matrix(r, layer, "node_first"))
    hidden_in = hidden_in + vector(r, layer, "node_bias")
    r.zn[...] = hidden_in
    hidden = (hidden_in * sigmoid(hidden_in)).astype(BF)
    last = dot(hidden, matrix(r, layer, "node_second")) + vector(r, layer, "node_offset")
    r.pn[...] = last
    normal, _ = layer_norm(last)
    outlet = r.flag[...] * dot(summed, matrix(r, layer, "outlet_map"))
    latent = r.latent[...].astype(F32) + vector(r, layer, "node_gain") * normal + outlet
    r.latent_out[...] = latent
    if send:
        write_sent(r, latent.astype(BF), [r.send_rows[k : k + 1, :] for k in range(3)])


def returned_sum(r):
    spread = one_hot_rows([r.send_rows[k : k + 1, :] for k in range(3)], 512)
    back = jnp.concatenate([r.back0[...], r.back1[...], r.back2[...], r.back3[...]], axis=0)
    return dot(spread, back)


def backward_part(r, layer, grad, has_edge_grad, keep_edge_grad):
    own = r.latent[...].astype(BF)
    summed = r.half[...]
    hidden_in = r.zn[...]
    gate = sigmoid(hidden_in)
    hidden = (hidden_in * gate).astype(BF)
    normal, inverse = layer_norm(r.pn[...])
    r.vec[5:6, :] = jnp.sum(grad * normal, axis=0, keepdims=True)
    d_last = layer_norm_back(grad * vector(r, layer, "node_gain"), normal, inverse)
    r.vec[4:5, :] = jnp.sum(d_last, axis=0, keepdims=True)
    d_last = d_last.astype(BF)
    d_hidden = dot_nt(d_last, matrix(r, layer, "node_second")).astype(BF).astype(F32)
    d_in = d_hidden * (gate * (1.0 + hidden_in * (1.0 - gate)))
    r.vec[3:4, :] = jnp.sum(d_in, axis=0, keepdims=True)
    d_in = d_in.astype(BF)
    d_node_in = dot_nt(d_in, matrix(r, layer, "node_first"))
    d_outlet = (grad * r.flag[...]).astype(BF)
    d_summed = (d_node_in[:, 128:] + dot_nt(d_outlet, matrix(r, layer, "outlet_map"))).astype(BF)
    r.own2[:, 0:128] = d_summed[0:256]
    r.own2[:, 128:256] = d_summed[256:512]
    target = r.packed if layer == 0 else r.weights_out

    def put(start, value):
        count = value.shape[0] // 8
        target[start : start + count, 0:8, :] = value.reshape(count, 8, D).astype(BF)

    put(64, dot_tn(jnp.concatenate([own, summed], axis=1), d_in))
    put(96, dot_tn(hidden, d_last))
    put(112, dot_tn(summed, d_outlet))

    w1 = matrix(r, layer, "edge_first")
    w2 = matrix(r, layer, "edge_second")
    gain = vector(r, layer, "edge_gain")
    zero = jnp.zeros((1, D), F32)
    r.to_send[...] = jnp.zeros(r.to_send.shape, F32)
    r.to_recv[...] = jnp.zeros(r.to_recv.shape, F32)
    r.d_w2[...] = jnp.zeros((D, D), F32)
    r.d_w1[...] = jnp.zeros((D, D), F32)

    def chunk(c, carry):
        d_bias, d_offset, d_gain = carry
        rows = pl.ds(pl.multiple_of(c * CHUNK, CHUNK), CHUNK)
        upper = r.upper[rows, :] > 0.5
        outside = r.outside[rows, :] > 0.5
        picked = dot(r.hot_recv[rows, :], r.own2[...])
        d_message = jnp.where(upper, picked[:, 128:], picked[:, :128])
        if has_edge_grad:
            d_message = d_message + r.edge_grad[rows, :]
        live = d_message * r.alive[rows, :]
        normal, inverse = layer_norm(r.pre2[rows, :])
        d_gain = d_gain + jnp.sum(live * normal, axis=0, keepdims=True)
        d_second = layer_norm_back(live * gain, normal, inverse)
        d_offset = d_offset + jnp.sum(d_second, axis=0, keepdims=True)
        d_second = d_second.astype(BF)
        pre1 = r.z1[rows, :]
        gate = sigmoid(pre1)
        act = (pre1 * gate).astype(BF)
        d_act = dot_nt(d_second, w2).astype(BF).astype(F32)
        d_first = d_act * (gate * (1.0 + pre1 * (1.0 - gate)))
        d_bias = d_bias + jnp.sum(d_first, axis=0, keepdims=True)
        d_half = d_first.astype(BF)
        edge = r.edge[rows, :].astype(BF)
        r.d_w2[...] += dot_tn(act, d_second)
        r.d_w1[...] += dot_tn(edge, d_half)
        if keep_edge_grad:
            d_edge = dot_nt(d_half, w1[0:128]).astype(BF).astype(F32)
            r.edge_grad_out[rows, :] = d_edge + r.edge_grad[rows, :] if has_edge_grad else d_edge
        none = jnp.zeros((CHUNK, D), F32)
        split = jnp.concatenate([jnp.where(outside, none, d_first), jnp.where(outside, d_first, none)], axis=1)
        r.to_send[...] += dot(r.hot_send_t[:, rows], split.astype(BF))
        split = jnp.concatenate([jnp.where(upper, none, d_first), jnp.where(upper, d_first, none)], axis=1)
        r.to_recv[...] += dot(r.hot_half_t[:, rows], split.astype(BF))
        return d_bias, d_offset, d_gain

    d_bias, d_offset, d_gain = lax.fori_loop(0, 2048 // CHUNK, chunk, (zero, zero, zero))
    r.vec[0:1, :] = d_bias
    r.vec[1:2, :] = d_offset
    r.vec[2:3, :] = d_gain
    r.vec[6:8, :] = jnp.zeros((2, D), F32)
    from_own = r.to_send[:, 0:128].astype(BF)
    from_halo = r.to_send[0:384, 128:256].astype(BF)
    at_recv = jnp.concatenate([r.to_recv[:, 0:128], r.to_recv[:, 128:256]], axis=0).astype(BF)
    d_halo = dot_nt(from_halo, w1[128:256]).astype(BF)
    r.sent0[...] = d_halo[0:64]
    r.sent1[...] = d_halo[64:128]
    r.sent2[...] = d_halo[128:256]
    r.sent3[...] = d_halo[256:384]
    r.grad_out[...] = grad + d_node_in[:, 0:128] + dot_nt(from_own, w1[128:256]) + dot_nt(at_recv, w1[256:384])
    halo = jnp.concatenate([r.halo0[...], r.halo1[...], r.halo2[...], r.halo3[...]], axis=0)
    put(0, r.d_w1[...])
    put(16, dot_tn(own, from_own) + dot_tn(halo, from_halo))
    put(32, dot_tn(own, at_recv))
    put(48, r.d_w2[...])


def pack(r):
    for layer in (1, 2):
        r.packed[:, 8 * layer : 8 * layer + 8, :] = getattr(r, "weights%d" % layer)[...]
    vec = jnp.concatenate([r.vec[...], r.vec1[...], r.vec2[...]], axis=0)
    top = vec.astype(BF).astype(F32)
    rest = (vec - top).astype(BF).astype(F32)
    turned = jnp.transpose(jnp.concatenate([top, rest, jnp.zeros((80, D), F32)], axis=0))
    r.packed[:, 24:32, :] = jnp.broadcast_to(turned.reshape(128, 1, D), (128, 8, D)).astype(BF)


def middle(r):
    r.latent_grad[...] = r.top_grad[...] + returned_sum(r)
    total = jnp.sum(r.shares[...].astype(F32), axis=0)
    tail = total[24:25, :]
    top = tail.astype(BF).astype(F32)
    line = lax.broadcasted_iota(I32, (8, D), 0)
    tail = jnp.where(line == 0, top, jnp.where(line == 1, tail - top, 0.0))
    r.summed[...] = jnp.concatenate([total[0:24], tail], axis=0).astype(BF)


def finish(r):
    for layer in range(3):
        for name in MATRICES:
            first, count = PLACES[name]
            block = r.whole[first // 8 : (first + count) // 8, 8 * layer : 8 * layer + 8, :]
            getattr(r, name)[layer] = block.astype(F32).reshape(count, D)
    turned = jnp.transpose(jnp.sum(r.whole[:, 24:32, :].astype(F32), axis=1))
    vec = turned[0:24] + turned[24:48]
    for layer in range(3):
        for k, name in enumerate(VECTORS):
            getattr(r, name)[layer : layer + 1, :] = vec[8 * layer + k : 8 * layer + k + 1, :]


COPIED = ("edge", "senders", "receivers", "live", "flags", "top_grad")
PLACES = {
    "edge_first": (0, 384),
    "edge_second": (384, 128),
    "node_first": (512, 256),
    "node_second": (768, 128),
    "outlet_map": (896, 128),
}
SENT = [("sent0", (64, D), BF), ("sent1", (64, D), BF), ("sent2", (128, D), BF), ("sent3", (128, D), BF)]
LOADED = [
    ("edge", (2048, D), BF),
    ("top_grad", (512, D), F32),
    ("weights", (3, 1024, D), BF),
    ("vectors", (3, 8, D), F32),
    ("hot_send", (2048, 512), BF),
    ("hot_recv", (2048, 256), BF),
    ("hot_send_t", (512, 2048), BF),
    ("hot_recv_t", (512, 2048), BF),
    ("hot_half_t", (256, 2048), BF),
    ("outside", (2048, D), F32),
    ("upper", (2048, D), F32),
    ("alive", (2048, D), F32),
    ("flag", (512, D), F32),
]
FORWARD_USES = ("weights", "vectors", "hot_send", "hot_recv", "hot_recv_t", "outside", "upper", "alive", "flag")
BACKWARD_USES = ("weights", "vectors", "hot_recv", "hot_send_t", "hot_half_t", "outside", "upper", "alive", "flag")
FORWARD_SCRATCH = [("ext2", (512, 256), BF), ("total", (512, 256), F32)]
PAIR_SCRATCH = [("own2", (256, 256), BF)]
BACKWARD_SCRATCH = [
    ("to_send", (512, 256), F32),
    ("to_recv", (256, 256), F32),
    ("d_w1", (D, D), F32),
    ("d_w2", (D, D), F32),
]
RESIDUALS = [
    ("z1", (2048, D), F32),
    ("pre2", (2048, D), F32),
    ("zn", (512, D), F32),
    ("pn", (512, D), F32),
    ("half", (512, D), BF),
]


def pairs(axis, odd):
    count = lax.axis_size(axis)
    steps = []
    for low in range(odd, count - 1, 2):
        steps += [(low, low + 1), (low + 1, low)]
    return steps


def exchange(made, names):
    moved = []
    for k, (axis, odd) in enumerate((("sub", 0), ("sub", 1), ("dom", 0), ("dom", 1))):
        moved.append(lax.ppermute(made["sent%d" % k], axis, pairs(axis, odd)))
    return [(names + str(k), moved[k]) for k in range(4)]


ORDER = (
    "edge_first",
    "edge_bias",
    "edge_second",
    "edge_offset",
    "edge_gain",
    "node_first",
    "node_bias",
    "node_second",
    "node_offset",
    "node_gain",
    "outlet_map",
)


def on_device(nodes, edges, senders, receivers, edge_live, outlet_flags, send_rows, *rest):
    params = list(zip(ORDER, rest[:-1]))
    first = run(
        start_body,
        [("nodes_in", nodes), ("rows_in", send_rows.reshape(3, D))],
        SENT + [("send_rows", (3, D), I32)],
        [("nodes", (512, D), BF), ("rows", (3, D), I32), ("sem", (2,), None)],
        held=("nodes_in", "rows_in"),
    )
    raw = [
        ("edge_in", edges),
        ("senders_in", senders.reshape(16, D)),
        ("receivers_in", receivers.reshape(16, D)),
        ("live_in", edge_live.reshape(16, D)),
        ("flags_in", outlet_flags.reshape(4, D)),
        ("top_grad_in", rest[-1]),
    ] + params
    loaded = run(
        load_body,
        raw,
        LOADED,
        [(name, (16, D), I32) for name in ("senders", "receivers", "live")]
        + [("flags", (4, D), I32)]
        + [(name + "_raw", value.shape, F32) for name, value in params]
        + [("sem", (len(raw),), None)],
        flops=4 << 30,
        held=[name for name, _ in raw],
    )
    forward_ins = [("send_rows", first["send_rows"])] + [(name, loaded[name]) for name in FORWARD_USES]
    backward_ins = [("send_rows", first["send_rows"])] + [(name, loaded[name]) for name in BACKWARD_USES]
    both_ins = forward_ins + [pair for pair in backward_ins if pair[0] not in ("send_rows",) + FORWARD_USES]
    made = first
    latent, edge = nodes, loaded["edge"]
    entered = []
    for layer in range(2):
        entry = exchange(made, "halo") + [("latent", latent), ("edge", edge)]

        def forward(r, layer=layer):
            forward_part(r, layer, True, True)

        made = run(
            forward,
            forward_ins + entry,
            SENT + [("latent_out", (512, D), F32), ("edge_out", (2048, D), F32)] + RESIDUALS,
            FORWARD_SCRATCH + PAIR_SCRATCH,
            flops=4 << 30,
        )
        entered.append(entry + [(name, made[name]) for name, _, _ in RESIDUALS])
        latent, edge = made["latent_out"], made["edge_out"]

    def turn(r):
        forward_part(r, 2, False, False)
        backward_part(r, 2, r.top_grad[...], False, True)

    gradient_outs = SENT + [("grad_out", (512, D), F32), ("vec", (8, D), F32)]
    share = [("weights_out", (128, 8, D), BF)]
    edge_grad = [("edge_grad_out", (2048, D), F32)]
    made = run(
        turn,
        both_ins + exchange(made, "halo") + [("latent", latent), ("edge", edge), ("top_grad", loaded["top_grad"])],
        gradient_outs + share + edge_grad + [("latent_out", (512, D), F32)],
        FORWARD_SCRATCH + PAIR_SCRATCH + BACKWARD_SCRATCH + RESIDUALS,
        flops=12 << 30,
    )
    latent_out = made["latent_out"]
    done = [("weights2", made["weights_out"]), ("vec2", made["vec"])]
    for layer in (1, 0):

        def backward(r, layer=layer):
            backward_part(r, layer, r.top_grad[...] + returned_sum(r), True, layer > 0)
            if layer == 0:
                pack(r)

        made = run(
            backward,
            backward_ins
            + entered[layer]
            + exchange(made, "back")
            + [("top_grad", made["grad_out"]), ("edge_grad", made["edge_grad_out"])]
            + ([] if layer else done),
            gradient_outs + (share + edge_grad if layer else [("packed", (128, 32, D), BF)]),
            PAIR_SCRATCH + BACKWARD_SCRATCH,
            flops=8 << 30,
        )
        if layer:
            done += [("weights1", made["weights_out"]), ("vec1", made["vec"])]

    back = exchange(made, "back")
    shares = lax.all_to_all(made["packed"], AXES, 0, 0, tiled=True)
    mid = run(
        middle,
        [("send_rows", first["send_rows"]), ("top_grad", made["grad_out"]), ("shares", shares)] + back,
        [("latent_grad", (512, D), F32), ("summed", (32, D), BF)],
    )
    spread = jnp.broadcast_to(mid["summed"][None], (128, 32, D))
    whole = lax.all_to_all(spread, AXES, 0, 0, tiled=True)
    results = run(finish, [("whole", whole)], [(name, value.shape, F32) for name, value in params])
    return (latent_out, mid["latent_grad"]) + tuple(results[name] for name in ORDER)


def solution(mesh):
    split = P(AXES, None)
    flat = P(AXES)
    placed = (split, split) + (flat,) * 5 + (P(),) * 11 + (split,)
    return jax.shard_map(
        on_device,
        mesh=mesh,
        in_specs=placed,
        out_specs=(split, split) + (P(),) * 11,
        check_vma=False,
    )
```

```python
import types

import jax
import jax.numpy as jnp
from jax import lax
from jax.experimental import pallas as pl
from jax.experimental.pallas import tpu as pltpu
from jax.sharding import Mesh, PartitionSpec as P

BF = jnp.bfloat16
F32 = jnp.float32
I32 = jnp.int32
D = 128
AXES = ("dom", "x", "core")
SUB = ("x", "core")
PEERS = ("dom", "x")
VMEM_LIMIT = 20 << 20

PLACES = dict(
    edge_first=(0, 384),
    edge_second=(384, 128),
    node_first=(512, 256),
    node_second=(768, 128),
    outlet_map=(896, 128),
)
LINES = dict(edge_bias=0, edge_offset=1, edge_gain=2, node_bias=3, node_offset=4, node_gain=5)


def dot(a, b):
    return jnp.dot(a, b, preferred_element_type=F32)


def dot_nt(a, b):
    return lax.dot_general(a, b, (((1,), (1,)), ((), ())), preferred_element_type=F32)


def dot_tn(a, b):
    return lax.dot_general(a, b, (((0,), (0,)), ((), ())), preferred_element_type=F32)


def sigmoid(x):
    return 0.5 * jnp.tanh(0.5 * x) + 0.5


def layer_norm(v):
    centered = v - jnp.mean(v, axis=-1, keepdims=True)
    inverse = lax.rsqrt(jnp.mean(centered * centered, axis=-1, keepdims=True) + 1e-05)
    return centered * inverse, inverse


def layer_norm_back(grad, normal, inverse):
    mean = jnp.mean(grad, axis=-1, keepdims=True)
    along = jnp.mean(grad * normal, axis=-1, keepdims=True)
    return inverse * (grad - mean - normal * along)


def one_hot_columns(index, count, unit=1):
    lane = lax.broadcasted_iota(I32, index.shape, 1) * unit
    parts = [jnp.where(index == lane + D * k * unit, 1.0, 0.0).astype(BF) for k in range(count)]
    return jnp.concatenate(parts, axis=1)


def one_hot_rows(rows, count):
    place = lax.broadcasted_iota(I32, (count, D), 0)
    parts = [jnp.where(place == row, 1.0, 0.0).astype(BF) for row in rows]
    return parts[0] if len(parts) == 1 else jnp.concatenate(parts, axis=1)


def column(row):
    corner = lax.broadcasted_iota(I32, (D, D), 0) == lax.broadcasted_iota(I32, (D, D), 1)
    total = jnp.sum(jnp.where(corner, jnp.broadcast_to(row, (D, D)), 0.0), axis=1, keepdims=True)
    return jnp.broadcast_to(total, (D, D))


def run(body, ins, outs, scratch=None, flops=0, held=False):
    scratch = scratch or {}
    names = [*ins, *outs, *scratch]

    def kernel(*refs):
        body(types.SimpleNamespace(**dict(zip(names, refs))))

    results = pl.pallas_call(
        kernel,
        out_shape=[jax.ShapeDtypeStruct(shape, dtype) for shape, dtype in outs.values()],
        in_specs=[pl.BlockSpec(memory_space=pltpu.HBM if held else pltpu.VMEM) for _ in ins],
        out_specs=[pl.BlockSpec(memory_space=pltpu.VMEM) for _ in outs],
        scratch_shapes=[
            pltpu.SemaphoreType.DMA(shape) if dtype is None else pltpu.VMEM(shape, dtype)
            for shape, dtype in scratch.values()
        ],
        compiler_params=pltpu.CompilerParams(vmem_limit_bytes=VMEM_LIMIT),
        cost_estimate=pl.CostEstimate(flops=flops, bytes_accessed=4 << 20, transcendentals=0),
    )(*[pltpu.with_memory_space_constraint(value, pltpu.HBM) if held else value for value in ins.values()])
    return dict(zip(outs, results))


VMEM_LIMIT = 20 << 20


def fetch(r, moves):
    copies = [pltpu.make_async_copy(source, target, r.sem.at[k]) for k, (source, target) in enumerate(moves)]
    for copy in copies:
        copy.start()
    return copies


def write_sent(r, own, rows):
    columns = [column(row.astype(F32)).astype(I32) for row in rows]
    picks = one_hot_columns(jnp.concatenate(columns, axis=0), 4)
    sent = dot(picks, own).astype(BF)
    r.sent0[...] = sent[0:64]
    r.sent1[...] = sent[64:128]
    r.sent2[...] = sent[128:256]
    r.sent3[...] = sent[256:384]


def even(axis):
    return lax.rem(lax.axis_index(axis), 2) == 0


def start_body(r):
    for copy in fetch(r, [(r.nodes_in, r.nodes), (r.rows_in, r.rows)]):
        copy.wait()
    sub_even, dom_even = even("core"), even("dom")
    row0, row1, row2 = (r.rows[k : k + 1, :] for k in range(3))
    turned = jnp.concatenate([row0[:, 64:], row0[:, :64]], axis=1)
    first = jnp.where(sub_even, turned, row0)
    second = jnp.where(dom_even, row2, row1)
    third = jnp.where(dom_even, row1, row2)
    r.send_rows[0:1, :] = first
    r.send_rows[1:2, :] = second
    r.send_rows[2:3, :] = third
    write_sent(r, r.nodes[...], (first, second, third))


def load_body(r):
    small = [
        (r.senders_in, r.senders),
        (r.receivers_in, r.receivers),
        (r.live_in, r.live),
        (r.flags_in, r.flags),
    ]
    large = [(r.edge_in, r.edge), (r.top_grad_in, r.top_grad)]
    large += [(getattr(r, name), getattr(r, name + "_raw")) for name in [*PLACES, *LINES]]
    copies = fetch(r, small + large)
    for copy in copies[: len(small)]:
        copy.wait()
    sub_even, dom_even = even("core"), even("dom")
    senders = r.senders[...]
    halo = senders - 512
    near = jnp.bitwise_xor(halo, jnp.where(sub_even, 64, 0)) + 512
    far = jnp.bitwise_xor(halo - 128, jnp.where(dom_even, 128, 0)) + 640
    senders = jnp.where(halo < 0, senders, jnp.where(halo < 128, near, far))
    receivers = r.receivers[...]
    places = jnp.bitwise_and(senders, 511)
    code = (senders + 1024 * receivers + (1024 * 512) * r.live[...]).astype(F32)
    for k in range(16):
        rows = slice(D * k, D * (k + 1))
        wide = one_hot_rows([receivers[k : k + 1, :]], 512)
        r.hot_send_t[:, rows] = one_hot_rows([places[k : k + 1, :]], 512)
        r.hot_recv_t[:, rows] = wide
        r.hot_half_t[:, rows] = wide[0:256] + wide[256:512]
        at = column(code[k : k + 1, :]).astype(I32)
        r.hot_send[rows, :] = one_hot_columns(jnp.bitwise_and(at, 511), 4)
        r.hot_recv[rows, :] = one_hot_columns(jnp.bitwise_and(at, 255 * 1024), 2, 1024)
        r.outside[rows, :] = jnp.bitwise_and(at, 512).astype(F32)
        r.upper[rows, :] = jnp.bitwise_and(at, 256 * 1024).astype(F32)
        r.alive[rows, :] = jnp.where(at >= 1024 * 512, 1.0, 0.0)
    for k in range(4):
        r.flag[D * k : D * (k + 1), :] = column(r.flags[k : k + 1, :].astype(F32))
    for copy in copies[len(small) :]:
        copy.wait()
    for layer in range(3):
        for name, (start, count) in PLACES.items():
            r.weights[layer, start : start + count, :] = getattr(r, name + "_raw")[layer].astype(BF)
        for name, k in LINES.items():
            r.vectors[layer, k : k + 1, :] = getattr(r, name + "_raw")[layer : layer + 1, :]


def gather_setup(r, own):
    r.ext2[:, 0:128] = own
    r.ext2[0:64, 128:256] = r.halo0[...]
    r.ext2[64:128, 128:256] = r.halo1[...]
    r.ext2[128:256, 128:256] = r.halo2[...]
    r.ext2[256:384, 128:256] = r.halo3[...]
    r.ext2[384:512, 128:256] = jnp.zeros((128, 128), BF)


def matrix(r, layer, name):
    first, count = PLACES[name]
    return r.weights[layer, first : first + count, :]


def vector(r, layer, name):
    k = LINES[name]
    return r.vectors[layer, k : k + 1, :]


def forward_part(r, layer, keep_edges, send):
    own = r.latent[...].astype(BF)
    gather_setup(r, own)
    r.own2[:, 0:128] = own[0:256]
    r.own2[:, 128:256] = own[256:512]
    w1 = matrix(r, layer, "edge_first")
    w2 = matrix(r, layer, "edge_second")
    b1 = vector(r, layer, "edge_bias")
    b2 = vector(r, layer, "edge_offset")
    gain = vector(r, layer, "edge_gain")
    picked = dot(r.hot_send[...], r.ext2[...])
    from_sender = jnp.where(r.outside[...] > 0.5, picked[:, 128:], picked[:, :128]).astype(BF)
    picked = dot(r.hot_recv[...], r.own2[...])
    at_receiver = jnp.where(r.upper[...] > 0.5, picked[:, 128:], picked[:, :128]).astype(BF)
    edge = r.edge[...].astype(F32)
    joined = jnp.concatenate([edge.astype(BF), from_sender, at_receiver], axis=1)
    pre1 = dot(joined, w1) + b1
    r.z1[...] = pre1
    act = (pre1 * sigmoid(pre1)).astype(BF)
    second = dot(act, w2) + b2
    r.pre2[...] = second
    normal, _ = layer_norm(second)
    message = r.alive[...] * gain * normal
    if keep_edges:
        r.edge_out[...] = edge + message
    top = message.astype(BF)
    rest = (message - top.astype(F32)).astype(BF)
    total = dot(r.hot_recv_t[...], jnp.concatenate([top, rest], axis=1))
    summed = (total[:, 0:128] + total[:, 128:256]).astype(BF)
    r.half[...] = summed
    hidden_in = dot(jnp.concatenate([own, summed], axis=1), matrix(r, layer, "node_first"))
    hidden_in = hidden_in + vector(r, layer, "node_bias")
    r.zn[...] = hidden_in
    hidden = (hidden_in * sigmoid(hidden_in)).astype(BF)
    last = dot(hidden, matrix(r, layer, "node_second")) + vector(r, layer, "node_offset")
    r.pn[...] = last
    normal, _ = layer_norm(last)
    outlet = r.flag[...] * dot(summed, matrix(r, layer, "outlet_map"))
    latent = r.latent[...].astype(F32) + vector(r, layer, "node_gain") * normal + outlet
    r.latent_out[...] = latent
    if send:
        write_sent(r, latent.astype(BF), [r.send_rows[k : k + 1, :] for k in range(3)])


def returned_sum(r):
    spread = one_hot_rows([r.send_rows[k : k + 1, :] for k in range(3)], 512)
    back = jnp.concatenate([r.back0[...], r.back1[...], r.back2[...], r.back3[...]], axis=0)
    return dot(spread, back)


def backward_part(r, layer, grad, has_edge_grad, keep_edge_grad):
    own = r.latent[...].astype(BF)
    summed = r.half[...]
    hidden_in = r.zn[...]
    gate = sigmoid(hidden_in)
    hidden = (hidden_in * gate).astype(BF)
    normal, inverse = layer_norm(r.pn[...])
    r.vec[5:6, :] = jnp.sum(grad * normal, axis=0, keepdims=True)
    d_last = layer_norm_back(grad * vector(r, layer, "node_gain"), normal, inverse)
    r.vec[4:5, :] = jnp.sum(d_last, axis=0, keepdims=True)
    d_last = d_last.astype(BF)
    d_hidden = dot_nt(d_last, matrix(r, layer, "node_second")).astype(BF).astype(F32)
    d_in = d_hidden * (gate * (1.0 + hidden_in * (1.0 - gate)))
    r.vec[3:4, :] = jnp.sum(d_in, axis=0, keepdims=True)
    d_in = d_in.astype(BF)
    d_node_in = dot_nt(d_in, matrix(r, layer, "node_first"))
    d_outlet = (grad * r.flag[...]).astype(BF)
    d_summed = (d_node_in[:, 128:] + dot_nt(d_outlet, matrix(r, layer, "outlet_map"))).astype(BF)
    r.own2[:, 0:128] = d_summed[0:256]
    r.own2[:, 128:256] = d_summed[256:512]
    target = r.packed if layer == 0 else r.weights_out

    def put(start, value):
        count = value.shape[0] // 8
        target[start : start + count, 0:8, :] = value.reshape(count, 8, D).astype(BF)

    put(64, dot_tn(jnp.concatenate([own, summed], axis=1), d_in))
    put(96, dot_tn(hidden, d_last))
    put(112, dot_tn(summed, d_outlet))

    w1 = matrix(r, layer, "edge_first")
    w2 = matrix(r, layer, "edge_second")
    gain = vector(r, layer, "edge_gain")
    upper = r.upper[...] > 0.5
    outside = r.outside[...] > 0.5
    picked = dot(r.hot_recv[...], r.own2[...])
    d_message = jnp.where(upper, picked[:, 128:], picked[:, :128])
    if has_edge_grad:
        d_message = d_message + r.edge_grad[...]
    live = d_message * r.alive[...]
    normal, inverse = layer_norm(r.pre2[...])
    r.vec[2:3, :] = jnp.sum(live * normal, axis=0, keepdims=True)
    d_second = layer_norm_back(live * gain, normal, inverse)
    r.vec[1:2, :] = jnp.sum(d_second, axis=0, keepdims=True)
    d_second = d_second.astype(BF)
    pre1 = r.z1[...]
    gate = sigmoid(pre1)
    act = (pre1 * gate).astype(BF)
    d_act = dot_nt(d_second, w2).astype(BF).astype(F32)
    d_first = d_act * (gate * (1.0 + pre1 * (1.0 - gate)))
    r.vec[0:1, :] = jnp.sum(d_first, axis=0, keepdims=True)
    d_half = d_first.astype(BF)
    edge = r.edge[...].astype(BF)
    put(48, dot_tn(act, d_second))
    put(0, dot_tn(edge, d_half))
    if keep_edge_grad:
        d_edge = dot_nt(d_half, w1[0:128]).astype(BF).astype(F32)
        r.edge_grad_out[...] = d_edge + r.edge_grad[...] if has_edge_grad else d_edge
    none = jnp.zeros((2048, D), F32)
    split = jnp.concatenate([jnp.where(outside, none, d_first), jnp.where(outside, d_first, none)], axis=1)
    to_send = dot(r.hot_send_t[...], split.astype(BF))
    split = jnp.concatenate([jnp.where(upper, none, d_first), jnp.where(upper, d_first, none)], axis=1)
    to_recv = dot(r.hot_half_t[...], split.astype(BF))
    r.vec[6:8, :] = jnp.zeros((2, D), F32)
    from_own = to_send[:, 0:128].astype(BF)
    from_halo = to_send[0:384, 128:256].astype(BF)
    at_recv = jnp.concatenate([to_recv[:, 0:128], to_recv[:, 128:256]], axis=0).astype(BF)
    d_halo = dot_nt(from_halo, w1[128:256]).astype(BF)
    r.sent0[...] = d_halo[0:64]
    r.sent1[...] = d_halo[64:128]
    r.sent2[...] = d_halo[128:256]
    r.sent3[...] = d_halo[256:384]
    r.grad_out[...] = grad + d_node_in[:, 0:128] + dot_nt(from_own, w1[128:256]) + dot_nt(at_recv, w1[256:384])
    halo = jnp.concatenate([r.halo0[...], r.halo1[...], r.halo2[...], r.halo3[...]], axis=0)
    put(16, dot_tn(own, from_own) + dot_tn(halo, from_halo))
    put(32, dot_tn(own, at_recv))


def pack(r):
    for layer, block in ((1, r.weights1), (2, r.weights2)):
        r.packed[:, 8 * layer : 8 * layer + 8, :] = block[...]
    vec = jnp.concatenate([r.vec[...], r.vec1[...], r.vec2[...]], axis=0)
    top = vec.astype(BF).astype(F32)
    rest = (vec - top).astype(BF).astype(F32)
    turned = jnp.transpose(jnp.concatenate([top, rest, jnp.zeros((80, D), F32)], axis=0))
    turned = jnp.broadcast_to(turned.reshape(128, 1, D), (128, 8, D))
    r.packed[:, 24:32, :] = jnp.where(lax.broadcasted_iota(I32, turned.shape, 1) == 0, turned, 0.0).astype(BF)
    r.given[...] = r.packed[pl.ds(64 * (1 - lax.axis_index("core")), 64)]


def two_terms(block):
    axis = block.ndim - 2
    value = jnp.sum(block, axis=axis, keepdims=True)
    top = value.astype(BF).astype(F32)
    line = lax.broadcasted_iota(I32, block.shape, axis)
    return jnp.where(line == 0, top, jnp.where(line == 1, value - top, 0.0)).astype(BF)


def pair_sum(r):
    total = r.packed[pl.ds(64 * lax.axis_index("core"), 64)].astype(F32) + r.got[...].astype(F32)
    r.chip[:, 0:24, :] = total[:, 0:24].astype(BF)
    r.chip[:, 24:32, :] = two_terms(total[:, 24:32])


def middle(r):
    r.latent_grad[...] = r.top_grad[...] + returned_sum(r)
    total = jnp.sum(r.shares[...].astype(F32), axis=0)
    r.summed[0:24, :] = total[0:24].astype(BF)
    r.summed[24:32, :] = two_terms(total[24:32])


def finish(r):
    core = lax.axis_index("core")
    r.whole[pl.ds(64 * core, 64)] = r.mine[...]
    r.whole[pl.ds(64 * (1 - core), 64)] = r.other[...]
    for layer in range(3):
        for name, (first, count) in PLACES.items():
            block = r.whole[first // 8 : (first + count) // 8, 8 * layer : 8 * layer + 8, :]
            getattr(r, name)[layer] = block.astype(F32).reshape(count, D)
    turned = jnp.transpose(jnp.sum(r.whole[:, 24:32, :].astype(F32), axis=1))
    vec = turned[0:24] + turned[24:48]
    for layer in range(3):
        for name, k in LINES.items():
            getattr(r, name)[layer : layer + 1, :] = vec[8 * layer + k : 8 * layer + k + 1, :]


SENT = dict(sent0=((64, D), BF), sent1=((64, D), BF), sent2=((128, D), BF), sent3=((128, D), BF))
LOADED = dict(
    edge=((2048, D), BF),
    top_grad=((512, D), F32),
    weights=((3, 1024, D), BF),
    vectors=((3, 8, D), F32),
    hot_send=((2048, 512), BF),
    hot_recv=((2048, 256), BF),
    hot_send_t=((512, 2048), BF),
    hot_recv_t=((512, 2048), BF),
    hot_half_t=((256, 2048), BF),
    outside=((2048, D), F32),
    upper=((2048, D), F32),
    alive=((2048, D), F32),
    flag=((512, D), F32),
)
FORWARD_SCRATCH = dict(ext2=((512, 256), BF))
PAIR_SCRATCH = dict(own2=((256, 256), BF))
RESIDUALS = dict(
    z1=((2048, D), F32),
    pre2=((2048, D), F32),
    zn=((512, D), F32),
    pn=((512, D), F32),
    half=((512, D), BF),
)


def pairs(count, odd):
    steps = []
    for low in range(odd, count - 1, 2):
        steps += [(low, low + 1), (low + 1, low)]
    return steps


def exchange(made):
    sub = lax.axis_size("x") * lax.axis_size("core")
    dom = lax.axis_size("dom")
    far = lax.ppermute(made["sent1"], SUB, pairs(sub, 1))
    near = lax.ppermute(made["sent0"], SUB, pairs(sub, 0))
    return (
        near,
        far,
        lax.ppermute(made["sent2"], "dom", pairs(dom, 0)),
        lax.ppermute(made["sent3"], "dom", pairs(dom, 1)),
    )


def halo_of(made):
    h0, h1, h2, h3 = exchange(made)
    return dict(halo1=h1, halo0=h0, halo2=h2, halo3=h3)


def back_of(made):
    b0, b1, b2, b3 = exchange(made)
    return dict(back1=b1, back0=b0, back2=b2, back3=b3)


def on_device(
    nodes,
    edges,
    senders,
    receivers,
    edge_live,
    outlet_flags,
    send_rows,
    edge_first,
    edge_bias,
    edge_second,
    edge_offset,
    edge_gain,
    node_first,
    node_bias,
    node_second,
    node_offset,
    node_gain,
    outlet_map,
    grad_out,
):
    params = dict(
        edge_first=edge_first,
        edge_bias=edge_bias,
        edge_second=edge_second,
        edge_offset=edge_offset,
        edge_gain=edge_gain,
        node_first=node_first,
        node_bias=node_bias,
        node_second=node_second,
        node_offset=node_offset,
        node_gain=node_gain,
        outlet_map=outlet_map,
    )
    made = run(
        start_body,
        dict(nodes_in=nodes, rows_in=send_rows.reshape(3, D)),
        dict(SENT, send_rows=((3, D), I32)),
        dict(nodes=((512, D), BF), rows=((3, D), I32), sem=((2,), None)),
        held=True,
    )
    rows = dict(send_rows=made["send_rows"])
    raw = dict(
        edge_in=edges,
        senders_in=senders.reshape(16, D),
        receivers_in=receivers.reshape(16, D),
        live_in=edge_live.reshape(16, D),
        flags_in=outlet_flags.reshape(4, D),
        top_grad_in=grad_out,
        **params,
    )
    index = ((16, D), I32)
    table = run(
        load_body,
        raw,
        LOADED,
        dict(
            senders=index,
            receivers=index,
            live=index,
            flags=((4, D), I32),
            sem=((len(raw),), None),
            **{name + "_raw": (value.shape, F32) for name, value in params.items()},
        ),
        flops=4 << 30,
        held=True,
    )
    edge, top_grad = table.pop("edge"), table.pop("top_grad")
    forward_table = {name: table[name] for name in table if name not in dict(hot_send_t=0, hot_half_t=0)}
    backward_table = {name: table[name] for name in table if name not in dict(hot_send=0, hot_recv_t=0)}
    latent = nodes
    entered = []
    for layer in range(2):
        entry = dict(halo_of(made), latent=latent, edge=edge)

        def forward(r, layer=layer):
            forward_part(r, layer, True, True)

        made = run(
            forward,
            dict(rows, **forward_table, **entry),
            dict(SENT, latent_out=((512, D), F32), edge_out=((2048, D), F32), **RESIDUALS),
            dict(FORWARD_SCRATCH, **PAIR_SCRATCH),
            flops=4 << 30,
        )
        entered.append(dict(entry, **{name: made[name] for name in RESIDUALS}))
        latent, edge = made["latent_out"], made["edge_out"]

    def turn(r):
        forward_part(r, 2, False, False)
        backward_part(r, 2, r.top_grad[...], False, True)

    gradient = dict(SENT, grad_out=((512, D), F32), vec=((8, D), F32))
    share = dict(weights_out=((128, 8, D), BF), edge_grad_out=((2048, D), F32))
    made = run(
        turn,
        dict(table, **halo_of(made), latent=latent, edge=edge, top_grad=top_grad),
        dict(gradient, **share, latent_out=((512, D), F32)),
        dict(FORWARD_SCRATCH, **PAIR_SCRATCH, **RESIDUALS),
        flops=12 << 30,
    )
    latent_out = made["latent_out"]
    done = dict(weights2=made["weights_out"], vec2=made["vec"])

    def backward_one(r):
        backward_part(r, 1, r.top_grad[...] + returned_sum(r), True, True)

    made = run(
        backward_one,
        dict(
            rows,
            **backward_table,
            **entered[1],
            **back_of(made),
            top_grad=made["grad_out"],
            edge_grad=made["edge_grad_out"],
        ),
        dict(gradient, **share),
        PAIR_SCRATCH,
        flops=8 << 30,
    )
    done.update(weights1=made["weights_out"], vec1=made["vec"])

    def backward_zero(r):
        backward_part(r, 0, r.top_grad[...] + returned_sum(r), True, False)
        pack(r)

    made = run(
        backward_zero,
        dict(
            rows,
            **backward_table,
            **entered[0],
            **back_of(made),
            top_grad=made["grad_out"],
            edge_grad=made["edge_grad_out"],
            **done,
        ),
        dict(gradient, packed=((128, 32, D), BF), given=((64, 32, D), BF)),
        PAIR_SCRATCH,
        flops=8 << 30,
    )
    swap = [(0, 1), (1, 0)]
    got = lax.ppermute(made["given"], "core", swap)
    chip = run(pair_sum, dict(packed=made["packed"], got=got), dict(chip=((64, 32, D), BF)))["chip"]
    shares = lax.all_to_all(chip, PEERS, 0, 0, tiled=True)
    mid = run(
        middle,
        dict(rows, top_grad=made["grad_out"], shares=shares, **back_of(made)),
        dict(latent_grad=((512, D), F32), summed=((32, D), BF)),
    )
    spread = jnp.broadcast_to(mid["summed"][None], (64, 32, D))
    mine = lax.all_to_all(spread, PEERS, 0, 0, tiled=True)
    other = lax.ppermute(mine, "core", swap)
    results = run(
        finish,
        dict(mine=mine, other=other),
        {name: (value.shape, F32) for name, value in params.items()},
        dict(whole=((128, 32, D), BF)),
    )
    return (latent_out, mid["latent_grad"]) + tuple(results[name] for name in params)


def solution(mesh):
    inner = Mesh(mesh.devices.reshape(mesh.devices.shape[0], -1, 2), AXES)
    split = P(AXES, None)
    flat = P(AXES)
    placed = (split, split) + (flat,) * 5 + (P(),) * 11 + (split,)
    return jax.shard_map(
        on_device,
        mesh=inner,
        in_specs=placed,
        out_specs=(split, split) + (P(),) * 11,
        check_vma=False,
    )
```

```python
import types

import jax
import jax.numpy as jnp
from jax import lax
from jax.experimental import pallas as pl
from jax.experimental.pallas import tpu as pltpu
from jax.sharding import Mesh, PartitionSpec as P

BF = jnp.bfloat16
F32 = jnp.float32
I32 = jnp.int32
D = 128
CHUNK = 2048
AXES = ("dom", "x", "core")
SUB = ("x", "core")
PEERS = ("dom", "x")
VMEM_LIMIT = 20 << 20

PLACES = dict(
    edge_first=(0, 384),
    edge_second=(384, 128),
    node_first=(512, 256),
    node_second=(768, 128),
    outlet_map=(896, 128),
)
LINES = dict(edge_bias=0, edge_offset=1, edge_gain=2, node_bias=3, node_offset=4, node_gain=5)


def dot(a, b):
    return jnp.dot(a, b, preferred_element_type=F32)


def dot_nt(a, b):
    return lax.dot_general(a, b, (((1,), (1,)), ((), ())), preferred_element_type=F32)


def dot_tn(a, b):
    return lax.dot_general(a, b, (((0,), (0,)), ((), ())), preferred_element_type=F32)


def sigmoid(x):
    return 0.5 * jnp.tanh(0.5 * x) + 0.5


def layer_norm(v):
    centered = v - jnp.mean(v, axis=-1, keepdims=True)
    inverse = lax.rsqrt(jnp.mean(centered * centered, axis=-1, keepdims=True) + 1e-05)
    return centered * inverse, inverse


def layer_norm_back(grad, normal, inverse):
    mean = jnp.mean(grad, axis=-1, keepdims=True)
    along = jnp.mean(grad * normal, axis=-1, keepdims=True)
    return inverse * (grad - mean - normal * along)


def one_hot_columns(index, count, unit=1):
    lane = lax.broadcasted_iota(I32, index.shape, 1) * unit
    parts = [jnp.where(index == lane + D * k * unit, 1.0, 0.0).astype(BF) for k in range(count)]
    return jnp.concatenate(parts, axis=1)


def one_hot_rows(rows, count):
    place = lax.broadcasted_iota(I32, (count, D), 0)
    parts = [jnp.where(place == row, 1.0, 0.0).astype(BF) for row in rows]
    return parts[0] if len(parts) == 1 else jnp.concatenate(parts, axis=1)


def column(row):
    corner = lax.broadcasted_iota(I32, (D, D), 0) == lax.broadcasted_iota(I32, (D, D), 1)
    total = jnp.sum(jnp.where(corner, jnp.broadcast_to(row, (D, D)), 0.0), axis=1, keepdims=True)
    return jnp.broadcast_to(total, (D, D))


def run(body, ins, outs, scratch=None, flops=0, held=False):
    scratch = scratch or {}
    names = [*ins, *outs, *scratch]

    def kernel(*refs):
        body(types.SimpleNamespace(**dict(zip(names, refs))))

    results = pl.pallas_call(
        kernel,
        out_shape=[jax.ShapeDtypeStruct(shape, dtype) for shape, dtype in outs.values()],
        in_specs=[pl.BlockSpec(memory_space=pltpu.HBM if held else pltpu.VMEM) for _ in ins],
        out_specs=[pl.BlockSpec(memory_space=pltpu.VMEM) for _ in outs],
        scratch_shapes=[
            pltpu.SemaphoreType.DMA(shape) if dtype is None else pltpu.VMEM(shape, dtype)
            for shape, dtype in scratch.values()
        ],
        compiler_params=pltpu.CompilerParams(vmem_limit_bytes=VMEM_LIMIT),
        cost_estimate=pl.CostEstimate(flops=flops, bytes_accessed=4 << 20, transcendentals=0),
    )(*[pltpu.with_memory_space_constraint(value, pltpu.HBM) if held else value for value in ins.values()])
    return dict(zip(outs, results))


VMEM_LIMIT = 20 << 20


def fetch(r, moves):
    copies = [pltpu.make_async_copy(source, target, r.sem.at[k]) for k, (source, target) in enumerate(moves)]
    for copy in copies:
        copy.start()
    return copies


def write_sent(r, own):
    sent = dot(r.picks[...], own).astype(BF)
    r.sent0[...] = sent[0:128]
    r.sent1[...] = sent[0:128]
    r.sent2[...] = sent[128:256]
    r.sent3[...] = sent[256:384]


def even(axis):
    return lax.rem(lax.axis_index(axis), 2) == 0


def start_body(r):
    for copy in fetch(r, [(r.nodes_in, r.nodes), (r.rows_in, r.rows)]):
        copy.wait()
    sub_even, dom_even = even("core"), even("dom")
    row0, row1, row2 = (r.rows[k : k + 1, :] for k in range(3))
    turned = jnp.concatenate([row0[:, 64:], row0[:, :64]], axis=1)
    first = jnp.where(sub_even, turned, row0)
    second = jnp.where(dom_even, row2, row1)
    third = jnp.where(dom_even, row1, row2)
    for k, row in enumerate((first, second, third)):
        r.picks[D * k : D * (k + 1), :] = one_hot_columns(column(row.astype(F32)).astype(I32), 4)
        r.spread[:, D * k : D * (k + 1)] = one_hot_rows([row], 512)
    write_sent(r, r.nodes[...])


def load_body(r):
    small = [
        (r.senders_in, r.senders),
        (r.receivers_in, r.receivers),
        (r.live_in, r.live),
        (r.flags_in, r.flags),
    ]
    large = [(r.edge_in, r.edge), (r.top_grad_in, r.top_grad)]
    large += [(getattr(r, name), getattr(r, name + "_raw")) for name in [*PLACES, *LINES]]
    copies = fetch(r, small + large)
    for copy in copies[: len(small)]:
        copy.wait()
    sub_even, dom_even = even("core"), even("dom")
    senders = r.senders[...]
    halo = senders - 512
    near = jnp.bitwise_xor(halo, jnp.where(sub_even, 64, 0)) + 512
    far = jnp.bitwise_xor(halo - 128, jnp.where(dom_even, 128, 0)) + 640
    senders = jnp.where(halo < 0, senders, jnp.where(halo < 128, near, far))
    receivers = r.receivers[...]
    places = jnp.bitwise_and(senders, 511)
    code = (senders + 1024 * receivers + (1024 * 512) * r.live[...]).astype(F32)
    for k in range(16):
        rows = slice(D * k, D * (k + 1))
        wide = one_hot_rows([receivers[k : k + 1, :]], 512)
        r.hot_send_t[:, rows] = one_hot_rows([places[k : k + 1, :]], 512)
        r.hot_recv_t[:, rows] = wide
        r.hot_half_t[:, rows] = wide[0:256] + wide[256:512]
        at = column(code[k : k + 1, :]).astype(I32)
        r.hot_send[rows, :] = one_hot_columns(jnp.bitwise_and(at, 511), 4)
        r.hot_recv[rows, :] = one_hot_columns(jnp.bitwise_and(at, 255 * 1024), 2, 1024)
        r.outside[rows, :] = jnp.bitwise_and(at, 512).astype(F32)
        r.upper[rows, :] = jnp.bitwise_and(at, 256 * 1024).astype(F32)
        r.alive[rows, :] = jnp.where(at >= 1024 * 512, 1.0, 0.0)
    for k in range(4):
        r.flag[D * k : D * (k + 1), :] = column(r.flags[k : k + 1, :].astype(F32))
    for copy in copies[len(small) :]:
        copy.wait()
    for layer in range(3):
        for name, (start, count) in PLACES.items():
            r.weights[layer, start : start + count, :] = getattr(r, name + "_raw")[layer].astype(BF)
        for name, k in LINES.items():
            r.vectors[layer, k : k + 1, :] = getattr(r, name + "_raw")[layer : layer + 1, :]


def gather_setup(r, own):
    r.halo[0:64, :] = r.halo0[0:64, :]
    r.halo[64:128, :] = r.halo1[64:128, :]
    r.halo[128:256, :] = r.halo2[...]
    r.halo[256:384, :] = r.halo3[...]
    r.ext2[:, 0:128] = own
    r.ext2[0:384, 128:256] = r.halo[...]
    r.ext2[384:512, 128:256] = jnp.zeros((128, 128), BF)


def matrix(r, layer, name):
    first, count = PLACES[name]
    return r.weights[layer, first : first + count, :]


def vector(r, layer, name):
    k = LINES[name]
    return r.vectors[layer, k : k + 1, :]


def receiver_part(r, layer, own):
    r.own2[:, 0:128] = own[0:256]
    r.own2[:, 128:256] = own[256:512]
    w1 = matrix(r, layer, "edge_first")
    picked = dot(r.hot_recv[...], r.own2[...])
    at_receiver = jnp.where(r.upper[...] > 0.5, picked[:, 128:], picked[:, :128]).astype(BF)
    joined = jnp.concatenate([r.edge[...].astype(BF), at_receiver], axis=1)
    both = jnp.concatenate([w1[0:128], w1[256:384]], axis=0)
    return dot(joined, both) + vector(r, layer, "edge_bias")


def early(r, layer):
    r.part[...] = receiver_part(r, layer, r.latent[...].astype(BF))


def forward_part(r, layer, keep_edges, send, split):
    own = r.latent[...].astype(BF)
    gather_setup(r, own)
    if not split:
        r.own2[:, 0:128] = own[0:256]
        r.own2[:, 128:256] = own[256:512]
    w1 = matrix(r, layer, "edge_first")
    w2 = matrix(r, layer, "edge_second")
    b2 = vector(r, layer, "edge_offset")
    gain = vector(r, layer, "edge_gain")
    total = jnp.zeros((512, 256), F32)
    for start in range(0, 2048, CHUNK):
        rows = slice(start, start + CHUNK)
        picked = dot(r.hot_send[rows, :], r.ext2[...])
        from_sender = jnp.where(r.outside[rows, :] > 0.5, picked[:, 128:], picked[:, :128]).astype(BF)
        if split:
            pre1 = dot(from_sender, w1[128:256]) + r.part[rows, :]
        else:
            picked = dot(r.hot_recv[rows, :], r.own2[...])
            at_receiver = jnp.where(r.upper[rows, :] > 0.5, picked[:, 128:], picked[:, :128]).astype(BF)
            joined = jnp.concatenate([r.edge[rows, :].astype(BF), from_sender, at_receiver], axis=1)
            pre1 = dot(joined, w1) + vector(r, layer, "edge_bias")
        gate = sigmoid(pre1)
        act = pre1 * gate
        r.slope[rows, :] = gate + act * (1.0 - gate)
        act = act.astype(BF)
        r.act[rows, :] = act
        normal, inverse = layer_norm(dot(act, w2) + b2)
        r.normal[rows, :] = normal
        r.inverse[rows, :] = jnp.broadcast_to(inverse, normal.shape)
        message = r.alive[rows, :] * gain * normal
        if keep_edges:
            r.edge_out[rows, :] = r.edge[rows, :].astype(F32) + message
        top = message.astype(BF)
        rest = (message - top.astype(F32)).astype(BF)
        total = total + dot(r.hot_recv_t[:, rows], jnp.concatenate([top, rest], axis=1))
    summed = (total[:, 0:128] + total[:, 128:256]).astype(BF)
    r.half[...] = summed
    hidden_in = dot(jnp.concatenate([own, summed], axis=1), matrix(r, layer, "node_first"))
    hidden_in = hidden_in + vector(r, layer, "node_bias")
    r.zn[...] = hidden_in
    hidden = (hidden_in * sigmoid(hidden_in)).astype(BF)
    last = dot(hidden, matrix(r, layer, "node_second")) + vector(r, layer, "node_offset")
    r.pn[...] = last
    normal, _ = layer_norm(last)
    outlet = r.flag[...] * dot(summed, matrix(r, layer, "outlet_map"))
    latent = r.latent[...].astype(F32) + vector(r, layer, "node_gain") * normal + outlet
    r.latent_out[...] = latent
    if send:
        write_sent(r, latent.astype(BF))


def returned_sum(r):
    back = jnp.concatenate([r.back0[0:64], r.back1[64:128], r.back2[...], r.back3[...]], axis=0)
    return dot(r.spread[...], back)


def backward_part(r, layer, grad, has_edge_grad):
    own = r.latent[...].astype(BF)
    summed = r.half[...]
    hidden_in = r.zn[...]
    gate = sigmoid(hidden_in)
    hidden = (hidden_in * gate).astype(BF)
    normal, inverse = layer_norm(r.pn[...])
    r.vec[5:6, :] = jnp.sum(grad * normal, axis=0, keepdims=True)
    d_last = layer_norm_back(grad * vector(r, layer, "node_gain"), normal, inverse)
    r.vec[4:5, :] = jnp.sum(d_last, axis=0, keepdims=True)
    d_last = d_last.astype(BF)
    d_hidden = dot_nt(d_last, matrix(r, layer, "node_second")).astype(BF).astype(F32)
    d_in = d_hidden * (gate * (1.0 + hidden_in * (1.0 - gate)))
    r.vec[3:4, :] = jnp.sum(d_in, axis=0, keepdims=True)
    d_in = d_in.astype(BF)
    d_node_in = dot_nt(d_in, matrix(r, layer, "node_first"))
    d_outlet = (grad * r.flag[...]).astype(BF)
    d_summed = (d_node_in[:, 128:] + dot_nt(d_outlet, matrix(r, layer, "outlet_map"))).astype(BF)
    r.own2[:, 0:128] = d_summed[0:256]
    r.own2[:, 128:256] = d_summed[256:512]
    r.hidden[...] = hidden
    r.d_in[...] = d_in
    r.d_last[...] = d_last
    r.d_outlet[...] = d_outlet

    w1 = matrix(r, layer, "edge_first")
    w2 = matrix(r, layer, "edge_second")
    gain = vector(r, layer, "edge_gain")
    d_bias, d_offset, d_gain = (jnp.zeros((1, D), F32) for _ in range(3))
    to_send, to_recv = jnp.zeros((512, 256), F32), jnp.zeros((256, 256), F32)
    none = jnp.zeros((CHUNK, D), F32)
    for start in range(0, 2048, CHUNK):
        rows = slice(start, start + CHUNK)
        upper = r.upper[rows, :] > 0.5
        outside = r.outside[rows, :] > 0.5
        picked = dot(r.hot_recv[rows, :], r.own2[...])
        d_message = jnp.where(upper, picked[:, 128:], picked[:, :128])
        if has_edge_grad:
            d_message = d_message + r.edge_grad[rows, :]
        live = d_message * r.alive[rows, :]
        normal = r.normal[rows, :]
        d_gain = d_gain + jnp.sum(live * normal, axis=0, keepdims=True)
        d_second = layer_norm_back(live * gain, normal, r.inverse[rows, :])
        d_offset = d_offset + jnp.sum(d_second, axis=0, keepdims=True)
        d_second = d_second.astype(BF)
        d_act = dot_nt(d_second, w2).astype(BF).astype(F32)
        d_first = d_act * r.slope[rows, :]
        d_bias = d_bias + jnp.sum(d_first, axis=0, keepdims=True)
        d_half = d_first.astype(BF)
        r.d_second[rows, :] = d_second
        r.d_first[rows, :] = d_half
        split = jnp.concatenate([jnp.where(outside, none, d_first), jnp.where(outside, d_first, none)], axis=1)
        to_send = to_send + dot(r.hot_send_t[:, rows], split.astype(BF))
        split = jnp.concatenate([jnp.where(upper, none, d_first), jnp.where(upper, d_first, none)], axis=1)
        to_recv = to_recv + dot(r.hot_half_t[:, rows], split.astype(BF))
    r.vec[0:1, :] = d_bias
    r.vec[1:2, :] = d_offset
    r.vec[2:3, :] = d_gain
    r.vec[6:8, :] = jnp.zeros((2, D), F32)
    from_own = to_send[:, 0:128].astype(BF)
    from_halo = to_send[0:384, 128:256].astype(BF)
    at_recv = jnp.concatenate([to_recv[:, 0:128], to_recv[:, 128:256]], axis=0).astype(BF)
    d_halo = dot_nt(from_halo, w1[128:256]).astype(BF)
    r.sent0[...] = d_halo[0:128]
    r.sent1[...] = d_halo[0:128]
    r.sent2[...] = d_halo[128:256]
    r.sent3[...] = d_halo[256:384]
    r.grad_out[...] = grad + d_node_in[:, 0:128] + dot_nt(from_own, w1[128:256]) + dot_nt(at_recv, w1[256:384])
    r.from_own[...] = from_own
    r.from_halo[...] = from_halo
    r.at_recv[...] = at_recv


def late(r, layer, target, has_edge_grad, keep_edge_grad):
    def put(start, value):
        count = value.shape[0] // 8
        target[start : start + count, 0:8, :] = value.reshape(count, 8, D).astype(BF)

    own = r.latent[...].astype(BF)
    from_own, d_in = r.from_own[...], r.d_in[...]
    put(0, dot_tn(r.edge[...].astype(BF), r.d_first[...]))
    put(16, dot_tn(own, from_own) + dot_tn(r.halo[...], r.from_halo[...]))
    put(32, dot_tn(own, r.at_recv[...]))
    put(48, dot_tn(r.act[...], r.d_second[...]))
    put(64, dot_tn(jnp.concatenate([own, r.half[...]], axis=1), d_in))
    put(96, dot_tn(r.hidden[...], r.d_last[...]))
    put(112, dot_tn(r.half[...], r.d_outlet[...]))
    if keep_edge_grad:
        d_edge = dot_nt(r.d_first[...], matrix(r, layer, "edge_first")[0:128]).astype(BF).astype(F32)
        r.edge_grad_out[...] = d_edge + r.edge_grad[...] if has_edge_grad else d_edge


def pack(r):
    for layer, block in ((1, r.weights1), (2, r.weights2)):
        r.packed[:, 8 * layer : 8 * layer + 8, :] = block[...]
    vec = jnp.concatenate([r.vec[...], r.vec1[...], r.vec2[...]], axis=0)
    top = vec.astype(BF).astype(F32)
    rest = (vec - top).astype(BF).astype(F32)
    turned = jnp.transpose(jnp.concatenate([top, rest, jnp.zeros((80, D), F32)], axis=0))
    turned = jnp.broadcast_to(turned.reshape(128, 1, D), (128, 8, D))
    r.packed[:, 24:32, :] = jnp.where(lax.broadcasted_iota(I32, turned.shape, 1) == 0, turned, 0.0).astype(BF)
    r.given[...] = r.packed[pl.ds(64 * (1 - lax.axis_index("core")), 64)]


def two_terms(block):
    axis = block.ndim - 2
    value = jnp.sum(block, axis=axis, keepdims=True)
    top = value.astype(BF).astype(F32)
    line = lax.broadcasted_iota(I32, block.shape, axis)
    return jnp.where(line == 0, top, jnp.where(line == 1, value - top, 0.0)).astype(BF)


def pair_sum(r):
    total = r.packed[pl.ds(64 * lax.axis_index("core"), 64)].astype(F32) + r.got[...].astype(F32)
    r.chip[:, 0:24, :] = total[:, 0:24].astype(BF)
    r.chip[:, 24:32, :] = two_terms(total[:, 24:32])


def middle(r):
    r.latent_grad[...] = r.top_grad[...] + returned_sum(r)
    total = jnp.sum(r.shares[...].astype(F32), axis=0)
    r.summed[0:24, :] = total[0:24].astype(BF)
    r.summed[24:32, :] = two_terms(total[24:32])


def finish(r):
    core = lax.axis_index("core")
    r.whole[pl.ds(64 * core, 64)] = r.mine[...]
    r.whole[pl.ds(64 * (1 - core), 64)] = r.other[...]
    for layer in range(3):
        for name, (first, count) in PLACES.items():
            block = r.whole[first // 8 : (first + count) // 8, 8 * layer : 8 * layer + 8, :]
            getattr(r, name)[layer] = block.astype(F32).reshape(count, D)
    turned = jnp.transpose(jnp.sum(r.whole[:, 24:32, :].astype(F32), axis=1))
    vec = turned[0:24] + turned[24:48]
    for layer in range(3):
        for name, k in LINES.items():
            getattr(r, name)[layer : layer + 1, :] = vec[8 * layer + k : 8 * layer + k + 1, :]


SENT = dict(sent0=((128, D), BF), sent1=((128, D), BF), sent2=((128, D), BF), sent3=((128, D), BF))
LOADED = dict(
    edge=((2048, D), BF),
    top_grad=((512, D), F32),
    weights=((3, 1024, D), BF),
    vectors=((3, 8, D), F32),
    hot_send=((2048, 512), BF),
    hot_recv=((2048, 256), BF),
    hot_send_t=((512, 2048), BF),
    hot_recv_t=((512, 2048), BF),
    hot_half_t=((256, 2048), BF),
    outside=((2048, D), F32),
    upper=((2048, D), F32),
    alive=((2048, D), F32),
    flag=((512, D), F32),
)
FORWARD_SCRATCH = dict(ext2=((512, 256), BF))
PAIR_SCRATCH = dict(own2=((256, 256), BF))
RESIDUALS = dict(
    act=((2048, D), BF),
    slope=((2048, D), F32),
    normal=((2048, D), F32),
    inverse=((2048, D), F32),
    zn=((512, D), F32),
    pn=((512, D), F32),
    half=((512, D), BF),
    halo=((384, D), BF),
)
HANDED = dict(
    hidden=((512, D), BF),
    d_in=((512, D), BF),
    d_last=((512, D), BF),
    d_outlet=((512, D), BF),
    d_second=((2048, D), BF),
    d_first=((2048, D), BF),
    from_own=((512, D), BF),
    from_halo=((384, D), BF),
    at_recv=((512, D), BF),
)


def pairs(count, odd):
    steps = []
    for low in range(odd, count - 1, 2):
        steps += [(low, low + 1), (low + 1, low)]
    return steps


def exchange(made):
    sub = lax.axis_size("x") * lax.axis_size("core")
    dom = lax.axis_size("dom")
    far = lax.ppermute(made["sent1"], SUB, pairs(sub, 1))
    near = lax.ppermute(made["sent0"], SUB, pairs(sub, 0))
    return (
        near,
        far,
        lax.ppermute(made["sent2"], "dom", pairs(dom, 0)),
        lax.ppermute(made["sent3"], "dom", pairs(dom, 1)),
    )


def halo_of(made):
    h0, h1, h2, h3 = exchange(made)
    return dict(halo2=h2, halo3=h3, halo1=h1, halo0=h0)


def back_of(made):
    b0, b1, b2, b3 = exchange(made)
    return dict(back2=b2, back3=b3, back1=b1, back0=b0)


def on_device(
    nodes,
    edges,
    senders,
    receivers,
    edge_live,
    outlet_flags,
    send_rows,
    edge_first,
    edge_bias,
    edge_second,
    edge_offset,
    edge_gain,
    node_first,
    node_bias,
    node_second,
    node_offset,
    node_gain,
    outlet_map,
    grad_out,
):
    params = dict(
        edge_first=edge_first,
        edge_bias=edge_bias,
        edge_second=edge_second,
        edge_offset=edge_offset,
        edge_gain=edge_gain,
        node_first=node_first,
        node_bias=node_bias,
        node_second=node_second,
        node_offset=node_offset,
        node_gain=node_gain,
        outlet_map=outlet_map,
    )
    made = run(
        start_body,
        dict(nodes_in=nodes, rows_in=send_rows.reshape(3, D)),
        dict(SENT, picks=((384, 512), BF), spread=((512, 384), BF)),
        dict(nodes=((512, D), BF), rows=((3, D), I32), sem=((2,), None)),
        held=True,
    )
    picks, spread = dict(picks=made["picks"]), dict(spread=made["spread"])
    raw = dict(
        edge_in=edges,
        senders_in=senders.reshape(16, D),
        receivers_in=receivers.reshape(16, D),
        live_in=edge_live.reshape(16, D),
        flags_in=outlet_flags.reshape(4, D),
        top_grad_in=grad_out,
        **params,
    )
    index = ((16, D), I32)
    table = run(
        load_body,
        raw,
        LOADED,
        dict(
            senders=index,
            receivers=index,
            live=index,
            flags=((4, D), I32),
            sem=((len(raw),), None),
            **{name + "_raw": (value.shape, F32) for name, value in params.items()},
        ),
        flops=4 << 30,
        held=True,
    )
    edge, top_grad = table.pop("edge"), table.pop("top_grad")
    forward_table = {name: table[name] for name in table if name not in dict(hot_send_t=0, hot_half_t=0)}
    backward_table = {name: table[name] for name in table if name not in dict(hot_send=0, hot_recv_t=0)}
    latent = nodes
    entered = []
    part = {}

    def begin(layer, latent, edge):
        ins = {name: table[name] for name in dict(weights=0, vectors=0, hot_recv=0, upper=0)}
        return run(
            lambda r: early(r, layer),
            dict(ins, latent=latent, edge=edge),
            dict(part=((2048, D), F32)),
            PAIR_SCRATCH,
            flops=2 << 30,
        )

    for layer in range(2):
        entry = dict(latent=latent, edge=edge)

        def forward(r, layer=layer):
            forward_part(r, layer, True, True, layer > 0)

        made = run(
            forward,
            dict(picks, **forward_table, **entry, **halo_of(made), **part),
            dict(SENT, latent_out=((512, D), F32), edge_out=((2048, D), F32), **RESIDUALS),
            dict(FORWARD_SCRATCH, **PAIR_SCRATCH),
            flops=4 << 30,
        )
        entered.append(dict(entry, **{name: made[name] for name in RESIDUALS}))
        latent, edge = made["latent_out"], made["edge_out"]
        part = begin(layer + 1, latent, edge)

    def turn(r):
        forward_part(r, 2, False, False, True)
        backward_part(r, 2, r.top_grad[...], False)

    gradient = dict(SENT, grad_out=((512, D), F32), vec=((8, D), F32))
    share = dict(weights_out=((128, 8, D), BF), edge_grad_out=((2048, D), F32))
    late_uses = dict(act=0, half=0, halo=0)
    made = run(
        turn,
        dict(table, **halo_of(made), latent=latent, edge=edge, top_grad=top_grad, **part),
        dict(
            gradient,
            latent_out=((512, D), F32),
            **HANDED,
            **{name: RESIDUALS[name] for name in late_uses},
        ),
        dict(
            FORWARD_SCRATCH,
            **PAIR_SCRATCH,
            **{name: RESIDUALS[name] for name in RESIDUALS if name not in late_uses},
        ),
        flops=12 << 30,
    )
    latent_out = made["latent_out"]
    late_ins = dict(weights=table["weights"])
    two = run(
        lambda r: late(r, 2, r.weights_out, False, True),
        dict(late_ins, latent=latent, edge=edge, **{name: made[name] for name in [*HANDED, *late_uses]}),
        share,
        flops=4 << 30,
    )
    done = dict(weights2=two["weights_out"], vec2=made["vec"])

    def backward_one(r):
        backward_part(r, 1, r.top_grad[...] + returned_sum(r), True)

    made = run(
        backward_one,
        dict(
            spread,
            **backward_table,
            **entered[1],
            **back_of(made),
            top_grad=made["grad_out"],
            edge_grad=two["edge_grad_out"],
        ),
        dict(gradient, **HANDED),
        PAIR_SCRATCH,
        flops=8 << 30,
    )
    one = run(
        lambda r: late(r, 1, r.weights_out, True, True),
        dict(
            late_ins,
            edge_grad=two["edge_grad_out"],
            **{name: made[name] for name in HANDED},
            **{name: entered[1][name] for name in dict(late_uses, latent=0, edge=0)},
        ),
        share,
        flops=4 << 30,
    )
    done.update(weights1=one["weights_out"], vec1=made["vec"])

    def backward_zero(r):
        backward_part(r, 0, r.top_grad[...] + returned_sum(r), True)
        late(r, 0, r.packed, True, False)
        pack(r)

    made = run(
        backward_zero,
        dict(
            spread,
            **backward_table,
            **entered[0],
            **back_of(made),
            top_grad=made["grad_out"],
            edge_grad=one["edge_grad_out"],
            **done,
        ),
        dict(gradient, packed=((128, 32, D), BF), given=((64, 32, D), BF)),
        dict(PAIR_SCRATCH, **HANDED),
        flops=8 << 30,
    )
    swap = [(0, 1), (1, 0)]
    got = lax.ppermute(made["given"], "core", swap)
    chip = run(pair_sum, dict(packed=made["packed"], got=got), dict(chip=((64, 32, D), BF)))["chip"]
    shares = lax.all_to_all(chip, PEERS, 0, 0, tiled=True)
    mid = run(
        middle,
        dict(spread, top_grad=made["grad_out"], shares=shares, **back_of(made)),
        dict(latent_grad=((512, D), F32), summed=((32, D), BF)),
    )
    spread = jnp.broadcast_to(mid["summed"][None], (64, 32, D))
    mine = lax.all_to_all(spread, PEERS, 0, 0, tiled=True)
    other = lax.ppermute(mine, "core", swap)
    results = run(
        finish,
        dict(mine=mine, other=other),
        {name: (value.shape, F32) for name, value in params.items()},
        dict(whole=((128, 32, D), BF)),
    )
    return (latent_out, mid["latent_grad"]) + tuple(results[name] for name in params)


def solution(mesh):
    inner = Mesh(mesh.devices.reshape(mesh.devices.shape[0], -1, 2), AXES)
    split = P(AXES, None)
    flat = P(AXES)
    placed = (split, split) + (flat,) * 5 + (P(),) * 11 + (split,)
    return jax.shard_map(
        on_device,
        mesh=inner,
        in_specs=placed,
        out_specs=(split, split) + (P(),) * 11,
        check_vma=False,
    )
```

```python
import types

import jax
import jax.numpy as jnp
from jax import lax
from jax.experimental import pallas as pl
from jax.experimental.pallas import tpu as pltpu
from jax.sharding import Mesh, PartitionSpec as P

BF = jnp.bfloat16
F32 = jnp.float32
I32 = jnp.int32
I16 = jnp.int16
D = 128
CHUNK = 2048
AXES = ("dom", "x", "core")
SUB = ("x", "core")
PEERS = ("dom", "x")
VMEM_LIMIT = 20 << 20

PLACES = dict(
    edge_first=(0, 384),
    edge_second=(384, 128),
    node_first=(512, 256),
    node_second=(768, 128),
    outlet_map=(896, 128),
)
LINES = dict(edge_bias=0, edge_offset=1, edge_gain=2, node_bias=3, node_offset=4, node_gain=5)


def dot(a, b):
    return jnp.dot(a, b, preferred_element_type=F32)


def dot_nt(a, b):
    return lax.dot_general(a, b, (((1,), (1,)), ((), ())), preferred_element_type=F32)


def dot_tn(a, b):
    return lax.dot_general(a, b, (((0,), (0,)), ((), ())), preferred_element_type=F32)


def sigmoid(x):
    return 0.5 * jnp.tanh(0.5 * x) + 0.5


def layer_norm(v):
    centered = v - jnp.mean(v, axis=-1, keepdims=True)
    inverse = lax.rsqrt(jnp.mean(centered * centered, axis=-1, keepdims=True) + 1e-05)
    return centered * inverse, inverse


def layer_norm_back(grad, normal, inverse):
    mean = jnp.mean(grad, axis=-1, keepdims=True)
    along = jnp.mean(grad * normal, axis=-1, keepdims=True)
    return inverse * (grad - mean - normal * along)


def one_hot_columns(index, count, shift=0):
    index = lax.shift_right_logical(index, shift).astype(I16)
    lane = lax.broadcasted_iota(I32, index.shape, 1).astype(I16)
    one, none = jnp.ones(index.shape, BF), jnp.zeros(index.shape, BF)
    return jnp.concatenate([jnp.where(index == lane + I16(D * k), one, none) for k in range(count)], axis=1)


def one_hot_rows(rows, count):
    place = lax.broadcasted_iota(I32, (count, D), 0).astype(I16)
    one, none = jnp.ones((count, D), BF), jnp.zeros((count, D), BF)
    wide = [jnp.broadcast_to(row, (count, D)).astype(I16) for row in rows]
    parts = [jnp.where(place == row, one, none) for row in wide]
    return parts[0] if len(parts) == 1 else jnp.concatenate(parts, axis=1)


def column(row):
    corner = lax.broadcasted_iota(I32, (D, D), 0) == lax.broadcasted_iota(I32, (D, D), 1)
    total = jnp.sum(jnp.where(corner, jnp.broadcast_to(row, (D, D)), 0.0), axis=1, keepdims=True)
    return jnp.broadcast_to(total, (D, D))


def run(body, ins, outs, scratch=None, flops=0, held=False):
    scratch = scratch or {}
    names = [*ins, *outs, *scratch]

    def kernel(*refs):
        body(types.SimpleNamespace(**dict(zip(names, refs))))

    results = pl.pallas_call(
        kernel,
        out_shape=[jax.ShapeDtypeStruct(shape, dtype) for shape, dtype in outs.values()],
        in_specs=[pl.BlockSpec(memory_space=pltpu.HBM if held else pltpu.VMEM) for _ in ins],
        out_specs=[pl.BlockSpec(memory_space=pltpu.VMEM) for _ in outs],
        scratch_shapes=[
            pltpu.SemaphoreType.DMA(shape) if dtype is None else pltpu.VMEM(shape, dtype)
            for shape, dtype in scratch.values()
        ],
        compiler_params=pltpu.CompilerParams(vmem_limit_bytes=VMEM_LIMIT),
        cost_estimate=pl.CostEstimate(flops=flops, bytes_accessed=4 << 20, transcendentals=0),
    )(*[pltpu.with_memory_space_constraint(value, pltpu.HBM) if held else value for value in ins.values()])
    return dict(zip(outs, results))


VMEM_LIMIT = 20 << 20


def fetch(r, moves):
    copies = [pltpu.make_async_copy(source, target, r.sem.at[k]) for k, (source, target) in enumerate(moves)]
    for copy in copies:
        copy.start()
    return copies


def write_sent(r, own):
    sent = dot(r.picks[...], own).astype(BF)
    r.sent0[...] = sent[0:128]
    r.sent1[...] = sent[0:128]
    r.sent2[...] = sent[128:256]
    r.sent3[...] = sent[256:384]


def even(axis):
    return lax.rem(lax.axis_index(axis), 2) == 0


def start_body(r):
    for copy in fetch(r, [(r.nodes_in, r.nodes), (r.rows_in, r.rows)]):
        copy.wait()
    sub_even, dom_even = even("core"), even("dom")
    row0, row1, row2 = (r.rows[k : k + 1, :] for k in range(3))
    turned = jnp.concatenate([row0[:, 64:], row0[:, :64]], axis=1)
    first = jnp.where(sub_even, turned, row0)
    second = jnp.where(dom_even, row2, row1)
    third = jnp.where(dom_even, row1, row2)
    for k, row in enumerate((first, second, third)):
        r.picks[D * k : D * (k + 1), :] = one_hot_columns(column(row.astype(F32)).astype(I32), 4)
        r.spread[:, D * k : D * (k + 1)] = one_hot_rows([row], 512)
    write_sent(r, r.nodes[...])


def load_body(r):
    small = [
        (r.senders_in, r.senders),
        (r.receivers_in, r.receivers),
        (r.live_in, r.live),
        (r.flags_in, r.flags),
    ]
    large = [(r.edge_in, r.edge), (r.top_grad_in, r.top_grad)]
    large += [(getattr(r, name), getattr(r, name + "_raw")) for name in [*PLACES, *LINES]]
    copies = fetch(r, small + large)
    for copy in copies[: len(small)]:
        copy.wait()
    sub_even, dom_even = even("core"), even("dom")
    senders = r.senders[...]
    halo = senders - 512
    near = jnp.bitwise_xor(halo, jnp.where(sub_even, 64, 0)) + 512
    far = jnp.bitwise_xor(halo - 128, jnp.where(dom_even, 128, 0)) + 640
    senders = jnp.where(halo < 0, senders, jnp.where(halo < 128, near, far))
    receivers = r.receivers[...]
    places = jnp.bitwise_and(senders, 511)
    code = (senders + 1024 * receivers + (1024 * 512) * r.live[...]).astype(F32)
    for k in range(16):
        rows = slice(D * k, D * (k + 1))
        r.hot_send_t[:, rows] = one_hot_rows([places[k : k + 1, :]], 512)
        r.hot_half_t[:, rows] = one_hot_rows([jnp.bitwise_and(receivers[k : k + 1, :], 255)], 256)
        at = column(code[k : k + 1, :]).astype(I32)
        r.hot_send[rows, :] = one_hot_columns(jnp.bitwise_and(at, 511), 4)
        r.hot_recv[rows, :] = one_hot_columns(jnp.bitwise_and(at, 255 * 1024), 2, 10)
        upper = jnp.where(jnp.bitwise_and(at, 256 * 1024) > 0, 1.0, 0.0)
        r.outside[rows, :] = jnp.where(jnp.bitwise_and(at, 512) > 0, 1.0, 0.0).astype(BF)
        r.upper_half[rows, :] = upper.astype(BF)
        r.upper[rows, :] = upper
        r.alive[rows, :] = jnp.where(at >= 1024 * 512, 1.0, 0.0)
    for k in range(4):
        r.flag[D * k : D * (k + 1), :] = column(r.flags[k : k + 1, :].astype(F32))
    for copy in copies[len(small) :]:
        copy.wait()
    for layer in range(3):
        for name, (start, count) in PLACES.items():
            r.weights[layer, start : start + count, :] = getattr(r, name + "_raw")[layer].astype(BF)
        for name, k in LINES.items():
            r.vectors[layer, k : k + 1, :] = getattr(r, name + "_raw")[layer : layer + 1, :]


def gather_setup(r, own):
    r.halo[0:64, :] = r.halo0[0:64, :]
    r.halo[64:128, :] = r.halo1[64:128, :]
    r.halo[128:256, :] = r.halo2[...]
    r.halo[256:384, :] = r.halo3[...]
    r.ext2[:, 0:128] = own
    r.ext2[0:384, 128:256] = r.halo[...]
    r.ext2[384:512, 128:256] = jnp.zeros((128, 128), BF)


def matrix(r, layer, name):
    first, count = PLACES[name]
    return r.weights[layer, first : first + count, :]


def vector(r, layer, name):
    k = LINES[name]
    return r.vectors[layer, k : k + 1, :]


def receiver_part(r, layer, own):
    r.own2[:, 0:128] = own[0:256]
    r.own2[:, 128:256] = own[256:512]
    w1 = matrix(r, layer, "edge_first")
    picked = dot(r.hot_recv[...], r.own2[...]).astype(BF)
    at_receiver = jnp.where(r.upper_half[...] > BF(0.5), picked[:, 128:], picked[:, :128])
    joined = jnp.concatenate([r.edge[...].astype(BF), at_receiver], axis=1)
    both = jnp.concatenate([w1[0:128], w1[256:384]], axis=0)
    return dot(joined, both) + vector(r, layer, "edge_bias")


def early(r, layer):
    r.part[...] = receiver_part(r, layer, r.latent[...].astype(BF))


def forward_part(r, layer, keep_edges, send, split):
    own = r.latent[...].astype(BF)
    gather_setup(r, own)
    if not split:
        r.own2[:, 0:128] = own[0:256]
        r.own2[:, 128:256] = own[256:512]
    w1 = matrix(r, layer, "edge_first")
    w2 = matrix(r, layer, "edge_second")
    b2 = vector(r, layer, "edge_offset")
    gain = vector(r, layer, "edge_gain")
    total = jnp.zeros((256, 256), F32)
    for start in range(0, 2048, CHUNK):
        rows = slice(start, start + CHUNK)
        picked = dot(r.hot_send[rows, :], r.ext2[...]).astype(BF)
        from_sender = jnp.where(r.outside[rows, :] > BF(0.5), picked[:, 128:], picked[:, :128])
        if split:
            pre1 = dot(from_sender, w1[128:256]) + r.part[rows, :]
        else:
            picked = dot(r.hot_recv[rows, :], r.own2[...]).astype(BF)
            at_receiver = jnp.where(r.upper_half[rows, :] > BF(0.5), picked[:, 128:], picked[:, :128])
            joined = jnp.concatenate([r.edge[rows, :].astype(BF), from_sender, at_receiver], axis=1)
            pre1 = dot(joined, w1) + vector(r, layer, "edge_bias")
        gate = sigmoid(pre1)
        act = pre1 * gate
        r.slope[rows, :] = gate + act * (1.0 - gate)
        act = act.astype(BF)
        r.act[rows, :] = act
        normal, inverse = layer_norm(dot(act, w2) + b2)
        r.normal[rows, :] = normal
        r.inverse[rows, :] = jnp.broadcast_to(inverse, normal.shape)
        message = r.alive[rows, :] * gain * normal
        if keep_edges:
            r.edge_out[rows, :] = r.edge[rows, :].astype(F32) + message
        message = message.astype(BF)
        upper = r.upper_half[rows, :] > BF(0.5)
        none = jnp.zeros(message.shape, BF)
        sides = jnp.concatenate([jnp.where(upper, none, message), jnp.where(upper, message, none)], axis=1)
        total = total + dot(r.hot_half_t[:, rows], sides)
    summed = jnp.concatenate([total[:, 0:128], total[:, 128:256]], axis=0).astype(BF)
    r.half[...] = summed
    hidden_in = dot(jnp.concatenate([own, summed], axis=1), matrix(r, layer, "node_first"))
    hidden_in = hidden_in + vector(r, layer, "node_bias")
    r.zn[...] = hidden_in
    hidden = (hidden_in * sigmoid(hidden_in)).astype(BF)
    last = dot(hidden, matrix(r, layer, "node_second")) + vector(r, layer, "node_offset")
    r.pn[...] = last
    normal, _ = layer_norm(last)
    outlet = r.flag[...] * dot(summed, matrix(r, layer, "outlet_map"))
    latent = r.latent[...].astype(F32) + vector(r, layer, "node_gain") * normal + outlet
    r.latent_out[...] = latent
    if send:
        write_sent(r, latent.astype(BF))


def returned_sum(r):
    back = jnp.concatenate([r.back0[0:64], r.back1[64:128], r.back2[...], r.back3[...]], axis=0)
    return dot(r.spread[...], back)


def backward_part(r, layer, grad, has_edge_grad):
    own = r.latent[...].astype(BF)
    summed = r.half[...]
    hidden_in = r.zn[...]
    gate = sigmoid(hidden_in)
    hidden = (hidden_in * gate).astype(BF)
    normal, inverse = layer_norm(r.pn[...])
    r.vec[5:6, :] = jnp.sum(grad * normal, axis=0, keepdims=True)
    d_last = layer_norm_back(grad * vector(r, layer, "node_gain"), normal, inverse)
    r.vec[4:5, :] = jnp.sum(d_last, axis=0, keepdims=True)
    d_last = d_last.astype(BF)
    d_hidden = dot_nt(d_last, matrix(r, layer, "node_second")).astype(BF).astype(F32)
    d_in = d_hidden * (gate * (1.0 + hidden_in * (1.0 - gate)))
    r.vec[3:4, :] = jnp.sum(d_in, axis=0, keepdims=True)
    d_in = d_in.astype(BF)
    d_node_in = dot_nt(d_in, matrix(r, layer, "node_first"))
    d_outlet = (grad * r.flag[...]).astype(BF)
    d_summed = (d_node_in[:, 128:] + dot_nt(d_outlet, matrix(r, layer, "outlet_map"))).astype(BF)
    r.own2[:, 0:128] = d_summed[0:256]
    r.own2[:, 128:256] = d_summed[256:512]
    r.hidden[...] = hidden
    r.d_in[...] = d_in
    r.d_last[...] = d_last
    r.d_outlet[...] = d_outlet

    w1 = matrix(r, layer, "edge_first")
    w2 = matrix(r, layer, "edge_second")
    gain = vector(r, layer, "edge_gain")
    d_bias, d_offset, d_gain = (jnp.zeros((1, D), F32) for _ in range(3))
    to_send, to_recv = jnp.zeros((512, 256), F32), jnp.zeros((256, 256), F32)
    none = jnp.zeros((CHUNK, D), BF)
    for start in range(0, 2048, CHUNK):
        rows = slice(start, start + CHUNK)
        upper = r.upper[rows, :] > 0.5
        outside = r.outside[rows, :] > BF(0.5)
        upper_half = r.upper_half[rows, :] > BF(0.5)
        picked = dot(r.hot_recv[rows, :], r.own2[...])
        d_message = jnp.where(upper, picked[:, 128:], picked[:, :128])
        if has_edge_grad:
            d_message = d_message + r.edge_grad[rows, :]
        live = d_message * r.alive[rows, :]
        normal = r.normal[rows, :]
        d_gain = d_gain + jnp.sum(live * normal, axis=0, keepdims=True)
        d_second = layer_norm_back(live * gain, normal, r.inverse[rows, :])
        d_offset = d_offset + jnp.sum(d_second, axis=0, keepdims=True)
        d_second = d_second.astype(BF)
        d_act = dot_nt(d_second, w2).astype(BF).astype(F32)
        d_first = d_act * r.slope[rows, :]
        d_bias = d_bias + jnp.sum(d_first, axis=0, keepdims=True)
        d_half = d_first.astype(BF)
        r.d_second[rows, :] = d_second
        r.d_first[rows, :] = d_half
        split = jnp.concatenate([jnp.where(outside, none, d_half), jnp.where(outside, d_half, none)], axis=1)
        to_send = to_send + dot(r.hot_send_t[:, rows], split)
        split = jnp.concatenate([jnp.where(upper_half, none, d_half), jnp.where(upper_half, d_half, none)], axis=1)
        to_recv = to_recv + dot(r.hot_half_t[:, rows], split)
    r.vec[0:1, :] = d_bias
    r.vec[1:2, :] = d_offset
    r.vec[2:3, :] = d_gain
    r.vec[6:8, :] = jnp.zeros((2, D), F32)
    from_own = to_send[:, 0:128].astype(BF)
    from_halo = to_send[0:384, 128:256].astype(BF)
    at_recv = jnp.concatenate([to_recv[:, 0:128], to_recv[:, 128:256]], axis=0).astype(BF)
    d_halo = dot_nt(from_halo, w1[128:256]).astype(BF)
    r.sent0[...] = d_halo[0:128]
    r.sent1[...] = d_halo[0:128]
    r.sent2[...] = d_halo[128:256]
    r.sent3[...] = d_halo[256:384]
    r.grad_out[...] = grad + d_node_in[:, 0:128] + dot_nt(from_own, w1[128:256]) + dot_nt(at_recv, w1[256:384])
    r.from_own[...] = from_own
    r.from_halo[...] = from_halo
    r.at_recv[...] = at_recv


def late(r, layer, target, has_edge_grad, keep_edge_grad):
    def put(start, value):
        count = value.shape[0] // 8
        target[start : start + count, 0:8, :] = value.reshape(count, 8, D).astype(BF)

    own = r.latent[...].astype(BF)
    from_own, d_in = r.from_own[...], r.d_in[...]
    put(0, dot_tn(r.edge[...].astype(BF), r.d_first[...]))
    put(16, dot_tn(own, from_own) + dot_tn(r.halo[...], r.from_halo[...]))
    put(32, dot_tn(own, r.at_recv[...]))
    put(48, dot_tn(r.act[...], r.d_second[...]))
    put(64, dot_tn(jnp.concatenate([own, r.half[...]], axis=1), d_in))
    put(96, dot_tn(r.hidden[...], r.d_last[...]))
    put(112, dot_tn(r.half[...], r.d_outlet[...]))
    if keep_edge_grad:
        d_edge = dot_nt(r.d_first[...], matrix(r, layer, "edge_first")[0:128]).astype(BF).astype(F32)
        r.edge_grad_out[...] = d_edge + r.edge_grad[...] if has_edge_grad else d_edge


def pack(r):
    for layer, block in ((1, r.weights1), (2, r.weights2)):
        r.packed[:, 8 * layer : 8 * layer + 8, :] = block[...]
    vec = jnp.concatenate([r.vec[...], r.vec1[...], r.vec2[...]], axis=0)
    top = vec.astype(BF).astype(F32)
    rest = (vec - top).astype(BF).astype(F32)
    turned = jnp.transpose(jnp.concatenate([top, rest, jnp.zeros((80, D), F32)], axis=0))
    turned = jnp.broadcast_to(turned.reshape(128, 1, D), (128, 8, D))
    r.packed[:, 24:32, :] = jnp.where(lax.broadcasted_iota(I32, turned.shape, 1) == 0, turned, 0.0).astype(BF)
    r.given[...] = r.packed[pl.ds(64 * (1 - lax.axis_index("core")), 64)]


def two_terms(block):
    axis = block.ndim - 2
    value = jnp.sum(block, axis=axis, keepdims=True)
    top = value.astype(BF).astype(F32)
    line = lax.broadcasted_iota(I32, block.shape, axis)
    return jnp.where(line == 0, top, jnp.where(line == 1, value - top, 0.0)).astype(BF)


def pair_sum(r):
    total = r.packed[pl.ds(64 * lax.axis_index("core"), 64)].astype(F32) + r.got[...].astype(F32)
    r.chip[:, 0:24, :] = total[:, 0:24].astype(BF)
    r.chip[:, 24:32, :] = two_terms(total[:, 24:32])


def middle(r):
    r.latent_grad[...] = r.top_grad[...] + returned_sum(r)
    total = jnp.sum(r.shares[...].astype(F32), axis=0)
    r.summed[0:24, :] = total[0:24].astype(BF)
    r.summed[24:32, :] = two_terms(total[24:32])


def finish(r):
    core = lax.axis_index("core")
    r.whole[pl.ds(64 * core, 64)] = r.mine[...]
    r.whole[pl.ds(64 * (1 - core), 64)] = r.other[...]
    for layer in range(3):
        for name, (first, count) in PLACES.items():
            block = r.whole[first // 8 : (first + count) // 8, 8 * layer : 8 * layer + 8, :]
            getattr(r, name)[layer] = block.astype(F32).reshape(count, D)
    turned = jnp.transpose(jnp.sum(r.whole[:, 24:32, :].astype(F32), axis=1))
    vec = turned[0:24] + turned[24:48]
    for layer in range(3):
        for name, k in LINES.items():
            getattr(r, name)[layer : layer + 1, :] = vec[8 * layer + k : 8 * layer + k + 1, :]


SENT = dict(sent0=((128, D), BF), sent1=((128, D), BF), sent2=((128, D), BF), sent3=((128, D), BF))
LOADED = dict(
    edge=((2048, D), BF),
    top_grad=((512, D), F32),
    weights=((3, 1024, D), BF),
    vectors=((3, 8, D), F32),
    hot_send=((2048, 512), BF),
    hot_recv=((2048, 256), BF),
    hot_send_t=((512, 2048), BF),
    hot_half_t=((256, 2048), BF),
    outside=((2048, D), BF),
    upper=((2048, D), F32),
    upper_half=((2048, D), BF),
    alive=((2048, D), F32),
    flag=((512, D), F32),
)
FORWARD_SCRATCH = dict(ext2=((512, 256), BF))
PAIR_SCRATCH = dict(own2=((256, 256), BF))
RESIDUALS = dict(
    act=((2048, D), BF),
    slope=((2048, D), F32),
    normal=((2048, D), F32),
    inverse=((2048, D), F32),
    zn=((512, D), F32),
    pn=((512, D), F32),
    half=((512, D), BF),
    halo=((384, D), BF),
)
HANDED = dict(
    hidden=((512, D), BF),
    d_in=((512, D), BF),
    d_last=((512, D), BF),
    d_outlet=((512, D), BF),
    d_second=((2048, D), BF),
    d_first=((2048, D), BF),
    from_own=((512, D), BF),
    from_halo=((384, D), BF),
    at_recv=((512, D), BF),
)


def pairs(count, odd):
    steps = []
    for low in range(odd, count - 1, 2):
        steps += [(low, low + 1), (low + 1, low)]
    return steps


def exchange(made):
    sub = lax.axis_size("x") * lax.axis_size("core")
    dom = lax.axis_size("dom")
    far = lax.ppermute(made["sent1"], SUB, pairs(sub, 1))
    near = lax.ppermute(made["sent0"], SUB, pairs(sub, 0))
    return (
        near,
        far,
        lax.ppermute(made["sent2"], "dom", pairs(dom, 0)),
        lax.ppermute(made["sent3"], "dom", pairs(dom, 1)),
    )


def halo_of(made):
    h0, h1, h2, h3 = exchange(made)
    return dict(halo2=h2, halo3=h3, halo1=h1, halo0=h0)


def back_of(made):
    b0, b1, b2, b3 = exchange(made)
    return dict(back2=b2, back3=b3, back1=b1, back0=b0)


def on_device(
    nodes,
    edges,
    senders,
    receivers,
    edge_live,
    outlet_flags,
    send_rows,
    edge_first,
    edge_bias,
    edge_second,
    edge_offset,
    edge_gain,
    node_first,
    node_bias,
    node_second,
    node_offset,
    node_gain,
    outlet_map,
    grad_out,
):
    params = dict(
        edge_first=edge_first,
        edge_bias=edge_bias,
        edge_second=edge_second,
        edge_offset=edge_offset,
        edge_gain=edge_gain,
        node_first=node_first,
        node_bias=node_bias,
        node_second=node_second,
        node_offset=node_offset,
        node_gain=node_gain,
        outlet_map=outlet_map,
    )
    made = run(
        start_body,
        dict(nodes_in=nodes, rows_in=send_rows.reshape(3, D)),
        dict(SENT, picks=((384, 512), BF), spread=((512, 384), BF)),
        dict(nodes=((512, D), BF), rows=((3, D), I32), sem=((2,), None)),
        held=True,
    )
    picks, spread = dict(picks=made["picks"]), dict(spread=made["spread"])
    raw = dict(
        edge_in=edges,
        senders_in=senders.reshape(16, D),
        receivers_in=receivers.reshape(16, D),
        live_in=edge_live.reshape(16, D),
        flags_in=outlet_flags.reshape(4, D),
        top_grad_in=grad_out,
        **params,
    )
    index = ((16, D), I32)
    table = run(
        load_body,
        raw,
        LOADED,
        dict(
            senders=index,
            receivers=index,
            live=index,
            flags=((4, D), I32),
            sem=((len(raw),), None),
            **{name + "_raw": (value.shape, F32) for name, value in params.items()},
        ),
        flops=4 << 30,
        held=True,
    )
    edge, top_grad = table.pop("edge"), table.pop("top_grad")
    forward_table = {name: table[name] for name in table if name not in dict(hot_send_t=0)}
    backward_table = {name: table[name] for name in table if name not in dict(hot_send=0)}
    latent = nodes
    entered = []
    part = {}

    def begin(layer, latent, edge):
        ins = {name: table[name] for name in dict(weights=0, vectors=0, hot_recv=0, upper_half=0)}
        return run(
            lambda r: early(r, layer),
            dict(ins, latent=latent, edge=edge),
            dict(part=((2048, D), F32)),
            PAIR_SCRATCH,
            flops=2 << 30,
        )

    for layer in range(2):
        entry = dict(latent=latent, edge=edge)

        def forward(r, layer=layer):
            forward_part(r, layer, True, True, layer > 0)

        made = run(
            forward,
            dict(picks, **forward_table, **entry, **halo_of(made), **part),
            dict(SENT, latent_out=((512, D), F32), edge_out=((2048, D), F32), **RESIDUALS),
            dict(FORWARD_SCRATCH, **PAIR_SCRATCH),
            flops=4 << 30,
        )
        entered.append(dict(entry, **{name: made[name] for name in RESIDUALS}))
        latent, edge = made["latent_out"], made["edge_out"]
        part = begin(layer + 1, latent, edge)

    def turn(r):
        forward_part(r, 2, False, False, True)
        backward_part(r, 2, r.top_grad[...], False)

    gradient = dict(SENT, grad_out=((512, D), F32), vec=((8, D), F32))
    share = dict(weights_out=((128, 8, D), BF), edge_grad_out=((2048, D), F32))
    late_uses = dict(act=0, half=0, halo=0)
    made = run(
        turn,
        dict(table, **halo_of(made), latent=latent, edge=edge, top_grad=top_grad, **part),
        dict(
            gradient,
            latent_out=((512, D), F32),
            **HANDED,
            **{name: RESIDUALS[name] for name in late_uses},
        ),
        dict(
            FORWARD_SCRATCH,
            **PAIR_SCRATCH,
            **{name: RESIDUALS[name] for name in RESIDUALS if name not in late_uses},
        ),
        flops=12 << 30,
    )
    latent_out = made["latent_out"]
    late_ins = dict(weights=table["weights"])
    two = run(
        lambda r: late(r, 2, r.weights_out, False, True),
        dict(late_ins, latent=latent, edge=edge, **{name: made[name] for name in [*HANDED, *late_uses]}),
        share,
        flops=4 << 30,
    )
    done = dict(weights2=two["weights_out"], vec2=made["vec"])

    def backward_one(r):
        backward_part(r, 1, r.top_grad[...] + returned_sum(r), True)

    made = run(
        backward_one,
        dict(
            spread,
            **backward_table,
            **entered[1],
            **back_of(made),
            top_grad=made["grad_out"],
            edge_grad=two["edge_grad_out"],
        ),
        dict(gradient, **HANDED),
        PAIR_SCRATCH,
        flops=8 << 30,
    )
    one = run(
        lambda r: late(r, 1, r.weights_out, True, True),
        dict(
            late_ins,
            edge_grad=two["edge_grad_out"],
            **{name: made[name] for name in HANDED},
            **{name: entered[1][name] for name in dict(late_uses, latent=0, edge=0)},
        ),
        share,
        flops=4 << 30,
    )
    done.update(weights1=one["weights_out"], vec1=made["vec"])

    def backward_zero(r):
        backward_part(r, 0, r.top_grad[...] + returned_sum(r), True)
        late(r, 0, r.packed, True, False)
        pack(r)

    made = run(
        backward_zero,
        dict(
            spread,
            **backward_table,
            **entered[0],
            **back_of(made),
            top_grad=made["grad_out"],
            edge_grad=one["edge_grad_out"],
            **done,
        ),
        dict(gradient, packed=((128, 32, D), BF), given=((64, 32, D), BF)),
        dict(PAIR_SCRATCH, **HANDED),
        flops=8 << 30,
    )
    swap = [(0, 1), (1, 0)]
    got = lax.ppermute(made["given"], "core", swap)
    chip = run(pair_sum, dict(packed=made["packed"], got=got), dict(chip=((64, 32, D), BF)))["chip"]
    shares = lax.all_to_all(chip, PEERS, 0, 0, tiled=True)
    mid = run(
        middle,
        dict(spread, top_grad=made["grad_out"], shares=shares, **back_of(made)),
        dict(latent_grad=((512, D), F32), summed=((32, D), BF)),
    )
    spread = jnp.broadcast_to(mid["summed"][None], (64, 32, D))
    mine = lax.all_to_all(spread, PEERS, 0, 0, tiled=True)
    other = lax.ppermute(mine, "core", swap)
    results = run(
        finish,
        dict(mine=mine, other=other),
        {name: (value.shape, F32) for name, value in params.items()},
        dict(whole=((128, 32, D), BF)),
    )
    return (latent_out, mid["latent_grad"]) + tuple(results[name] for name in params)


def solution(mesh):
    inner = Mesh(mesh.devices.reshape(mesh.devices.shape[0], -1, 2), AXES)
    split = P(AXES, None)
    flat = P(AXES)
    placed = (split, split) + (flat,) * 5 + (P(),) * 11 + (split,)
    return jax.shard_map(
        on_device,
        mesh=inner,
        in_specs=placed,
        out_specs=(split, split) + (P(),) * 11,
        check_vma=False,
    )
```

```python
import types

import jax
import jax.numpy as jnp
from jax import lax
from jax.experimental import pallas as pl
from jax.experimental.pallas import tpu as pltpu
from jax.sharding import Mesh, PartitionSpec as P

BF = jnp.bfloat16
F32 = jnp.float32
I32 = jnp.int32
I16 = jnp.int16
D = 128
CHUNK = 2048
AXES = ("dom", "x", "core")
SUB = ("x", "core")
PEERS = ("dom", "x")
VMEM_LIMIT = 20 << 20

PLACES = dict(
    edge_first=(0, 384),
    edge_second=(384, 128),
    node_first=(512, 256),
    node_second=(768, 128),
    outlet_map=(896, 128),
)
LINES = dict(edge_bias=0, edge_offset=1, edge_gain=2, node_bias=3, node_offset=4, node_gain=5)


def dot(a, b):
    return jnp.dot(a, b, preferred_element_type=F32)


def dot_nt(a, b):
    return lax.dot_general(a, b, (((1,), (1,)), ((), ())), preferred_element_type=F32)


def dot_tn(a, b):
    return lax.dot_general(a, b, (((0,), (0,)), ((), ())), preferred_element_type=F32)


def sigmoid(x):
    return 0.5 * jnp.tanh(0.5 * x) + 0.5


def layer_norm(v):
    centered = v - jnp.mean(v, axis=-1, keepdims=True)
    inverse = lax.rsqrt(jnp.mean(centered * centered, axis=-1, keepdims=True) + 1e-05)
    return centered * inverse, inverse


def layer_norm_back(grad, normal, inverse):
    mean = jnp.mean(grad, axis=-1, keepdims=True)
    along = jnp.mean(grad * normal, axis=-1, keepdims=True)
    return inverse * (grad - mean - normal * along)


def one_hot_columns(index, count, shift=0):
    index = lax.shift_right_logical(index, shift).astype(I16)
    lane = lax.broadcasted_iota(I32, index.shape, 1).astype(I16)
    one, none = jnp.ones(index.shape, BF), jnp.zeros(index.shape, BF)
    return jnp.concatenate([jnp.where(index == lane + I16(D * k), one, none) for k in range(count)], axis=1)


def one_hot_rows(rows, count):
    place = lax.broadcasted_iota(I32, (count, D), 0).astype(I16)
    one, none = jnp.ones((count, D), BF), jnp.zeros((count, D), BF)
    wide = [jnp.broadcast_to(row, (count, D)).astype(I16) for row in rows]
    parts = [jnp.where(place == row, one, none) for row in wide]
    return parts[0] if len(parts) == 1 else jnp.concatenate(parts, axis=1)


def column(row):
    corner = lax.broadcasted_iota(I32, (D, D), 0) == lax.broadcasted_iota(I32, (D, D), 1)
    total = jnp.sum(jnp.where(corner, jnp.broadcast_to(row, (D, D)), 0.0), axis=1, keepdims=True)
    return jnp.broadcast_to(total, (D, D))


def run(body, ins, outs, scratch=None, flops=0, held=False):
    scratch = scratch or {}
    names = [*ins, *outs, *scratch]

    def kernel(*refs):
        body(types.SimpleNamespace(**dict(zip(names, refs))))

    results = pl.pallas_call(
        kernel,
        out_shape=[jax.ShapeDtypeStruct(shape, dtype) for shape, dtype in outs.values()],
        in_specs=[pl.BlockSpec(memory_space=pltpu.HBM if held else pltpu.VMEM) for _ in ins],
        out_specs=[pl.BlockSpec(memory_space=pltpu.VMEM) for _ in outs],
        scratch_shapes=[
            pltpu.SemaphoreType.DMA(shape) if dtype is None else pltpu.VMEM(shape, dtype)
            for shape, dtype in scratch.values()
        ],
        compiler_params=pltpu.CompilerParams(vmem_limit_bytes=VMEM_LIMIT),
        cost_estimate=pl.CostEstimate(flops=flops, bytes_accessed=4 << 20, transcendentals=0),
    )(*[pltpu.with_memory_space_constraint(value, pltpu.HBM) if held else value for value in ins.values()])
    return dict(zip(outs, results))


VMEM_LIMIT = 20 << 20


def fetch(r, moves):
    copies = [pltpu.make_async_copy(source, target, r.sem.at[k]) for k, (source, target) in enumerate(moves)]
    for copy in copies:
        copy.start()
    return copies


def write_sent(r, own):
    sent = dot(r.picks[...], own).astype(BF)
    r.sent0[...] = sent[0:128]
    r.sent1[...] = sent[0:128]
    r.sent2[...] = sent[128:256]
    r.sent3[...] = sent[256:384]


def even(axis):
    return lax.rem(lax.axis_index(axis), 2) == 0


def start_body(r):
    for copy in fetch(r, [(r.nodes_in, r.nodes), (r.rows_in, r.rows)]):
        copy.wait()
    sub_even, dom_even = even("core"), even("dom")
    row0, row1, row2 = (r.rows[k : k + 1, :] for k in range(3))
    turned = jnp.concatenate([row0[:, 64:], row0[:, :64]], axis=1)
    first = jnp.where(sub_even, turned, row0)
    second = jnp.where(dom_even, row2, row1)
    third = jnp.where(dom_even, row1, row2)
    for k, row in enumerate((first, second, third)):
        r.picks[D * k : D * (k + 1), :] = one_hot_columns(column(row.astype(F32)).astype(I32), 4)
        r.spread[:, D * k : D * (k + 1)] = one_hot_rows([row], 512)
    write_sent(r, r.nodes[...])


def load_body(r):
    small = [
        (r.senders_in, r.senders),
        (r.receivers_in, r.receivers),
        (r.live_in, r.live),
        (r.flags_in, r.flags),
    ]
    large = [(r.edge_in, r.edge), (r.top_grad_in, r.top_grad)]
    large += [(getattr(r, name), getattr(r, name + "_raw")) for name in [*PLACES, *LINES]]
    copies = fetch(r, small + large)
    for copy in copies[: len(small)]:
        copy.wait()
    sub_even, dom_even = even("core"), even("dom")
    senders = r.senders[...]
    halo = senders - 512
    near = jnp.bitwise_xor(halo, jnp.where(sub_even, 64, 0)) + 512
    far = jnp.bitwise_xor(halo - 128, jnp.where(dom_even, 128, 0)) + 640
    senders = jnp.where(halo < 0, senders, jnp.where(halo < 128, near, far))
    receivers = r.receivers[...]
    r.places[...] = jnp.bitwise_and(senders, 511)
    code = (senders + 1024 * receivers + (1024 * 512) * r.live[...]).astype(F32)
    for k in range(16):
        rows = slice(D * k, D * (k + 1))
        r.hot_half_t[:, rows] = one_hot_rows([jnp.bitwise_and(receivers[k : k + 1, :], 255)], 256)
        at = column(code[k : k + 1, :]).astype(I32)
        r.hot_send[rows, :] = one_hot_columns(jnp.bitwise_and(at, 511), 4)
        r.hot_recv[rows, :] = one_hot_columns(jnp.bitwise_and(at, 255 * 1024), 2, 10)
        upper = jnp.where(jnp.bitwise_and(at, 256 * 1024) > 0, 1.0, 0.0)
        r.outside[rows, :] = jnp.where(jnp.bitwise_and(at, 512) > 0, 1.0, 0.0).astype(BF)
        r.upper_half[rows, :] = upper.astype(BF)
        r.upper[rows, :] = upper
        r.alive[rows, :] = jnp.where(at >= 1024 * 512, 1.0, 0.0)
    for k in range(4):
        r.flag[D * k : D * (k + 1), :] = column(r.flags[k : k + 1, :].astype(F32))
    for copy in copies[len(small) :]:
        copy.wait()
    for layer in range(3):
        for name, (start, count) in PLACES.items():
            r.weights[layer, start : start + count, :] = getattr(r, name + "_raw")[layer].astype(BF)
        for name, k in LINES.items():
            r.vectors[layer, k : k + 1, :] = getattr(r, name + "_raw")[layer : layer + 1, :]


def place_body(r):
    for k in range(16):
        r.hot_send_t[:, D * k : D * (k + 1)] = one_hot_rows([r.places[k : k + 1, :]], 512)


def gather_setup(r, own):
    r.halo[0:64, :] = r.halo0[0:64, :]
    r.halo[64:128, :] = r.halo1[64:128, :]
    r.halo[128:256, :] = r.halo2[...]
    r.halo[256:384, :] = r.halo3[...]
    r.ext2[:, 0:128] = own
    r.ext2[0:384, 128:256] = r.halo[...]
    r.ext2[384:512, 128:256] = jnp.zeros((128, 128), BF)


def matrix(r, layer, name):
    first, count = PLACES[name]
    return r.weights[layer, first : first + count, :]


def vector(r, layer, name):
    k = LINES[name]
    return r.vectors[layer, k : k + 1, :]


def receiver_part(r, layer, own):
    r.own2[:, 0:128] = own[0:256]
    r.own2[:, 128:256] = own[256:512]
    w1 = matrix(r, layer, "edge_first")
    picked = dot(r.hot_recv[...], r.own2[...]).astype(BF)
    at_receiver = jnp.where(r.upper_half[...] > BF(0.5), picked[:, 128:], picked[:, :128])
    joined = jnp.concatenate([r.edge[...].astype(BF), at_receiver], axis=1)
    both = jnp.concatenate([w1[0:128], w1[256:384]], axis=0)
    return dot(joined, both) + vector(r, layer, "edge_bias")


def early(r, layer):
    r.part[...] = receiver_part(r, layer, r.latent[...].astype(BF))


def forward_part(r, layer, keep_edges, send, split):
    own = r.latent[...].astype(BF)
    gather_setup(r, own)
    if not split:
        r.own2[:, 0:128] = own[0:256]
        r.own2[:, 128:256] = own[256:512]
    w1 = matrix(r, layer, "edge_first")
    w2 = matrix(r, layer, "edge_second")
    b2 = vector(r, layer, "edge_offset")
    gain = vector(r, layer, "edge_gain")
    total = jnp.zeros((256, 256), F32)
    for start in range(0, 2048, CHUNK):
        rows = slice(start, start + CHUNK)
        picked = dot(r.hot_send[rows, :], r.ext2[...]).astype(BF)
        from_sender = jnp.where(r.outside[rows, :] > BF(0.5), picked[:, 128:], picked[:, :128])
        if split:
            pre1 = dot(from_sender, w1[128:256]) + r.part[rows, :]
        else:
            picked = dot(r.hot_recv[rows, :], r.own2[...]).astype(BF)
            at_receiver = jnp.where(r.upper_half[rows, :] > BF(0.5), picked[:, 128:], picked[:, :128])
            joined = jnp.concatenate([r.edge[rows, :].astype(BF), from_sender, at_receiver], axis=1)
            pre1 = dot(joined, w1) + vector(r, layer, "edge_bias")
        gate = sigmoid(pre1)
        act = pre1 * gate
        r.slope[rows, :] = gate + act * (1.0 - gate)
        act = act.astype(BF)
        r.act[rows, :] = act
        normal, inverse = layer_norm(dot(act, w2) + b2)
        r.normal[rows, :] = normal
        r.inverse[rows, :] = jnp.broadcast_to(inverse, normal.shape)
        message = r.alive[rows, :] * gain * normal
        if keep_edges:
            r.edge_out[rows, :] = r.edge[rows, :].astype(F32) + message
        message = message.astype(BF)
        upper = r.upper_half[rows, :] > BF(0.5)
        none = jnp.zeros(message.shape, BF)
        sides = jnp.concatenate([jnp.where(upper, none, message), jnp.where(upper, message, none)], axis=1)
        total = total + dot(r.hot_half_t[:, rows], sides)
    summed = jnp.concatenate([total[:, 0:128], total[:, 128:256]], axis=0).astype(BF)
    r.half[...] = summed
    hidden_in = dot(jnp.concatenate([own, summed], axis=1), matrix(r, layer, "node_first"))
    hidden_in = hidden_in + vector(r, layer, "node_bias")
    r.zn[...] = hidden_in
    hidden = (hidden_in * sigmoid(hidden_in)).astype(BF)
    last = dot(hidden, matrix(r, layer, "node_second")) + vector(r, layer, "node_offset")
    r.pn[...] = last
    normal, _ = layer_norm(last)
    outlet = r.flag[...] * dot(summed, matrix(r, layer, "outlet_map"))
    latent = r.latent[...].astype(F32) + vector(r, layer, "node_gain") * normal + outlet
    r.latent_out[...] = latent
    if send:
        write_sent(r, latent.astype(BF))


def returned_sum(r):
    back = jnp.concatenate([r.back0[0:64], r.back1[64:128], r.back2[...], r.back3[...]], axis=0)
    return dot(r.spread[...], back)


def backward_part(r, layer, grad, has_edge_grad):
    own = r.latent[...].astype(BF)
    summed = r.half[...]
    hidden_in = r.zn[...]
    gate = sigmoid(hidden_in)
    hidden = (hidden_in * gate).astype(BF)
    normal, inverse = layer_norm(r.pn[...])
    r.vec[5:6, :] = jnp.sum(grad * normal, axis=0, keepdims=True)
    d_last = layer_norm_back(grad * vector(r, layer, "node_gain"), normal, inverse)
    r.vec[4:5, :] = jnp.sum(d_last, axis=0, keepdims=True)
    d_last = d_last.astype(BF)
    d_hidden = dot_nt(d_last, matrix(r, layer, "node_second")).astype(BF).astype(F32)
    d_in = d_hidden * (gate * (1.0 + hidden_in * (1.0 - gate)))
    r.vec[3:4, :] = jnp.sum(d_in, axis=0, keepdims=True)
    d_in = d_in.astype(BF)
    d_node_in = dot_nt(d_in, matrix(r, layer, "node_first"))
    d_outlet = (grad * r.flag[...]).astype(BF)
    d_summed = (d_node_in[:, 128:] + dot_nt(d_outlet, matrix(r, layer, "outlet_map"))).astype(BF)
    r.own2[:, 0:128] = d_summed[0:256]
    r.own2[:, 128:256] = d_summed[256:512]
    r.hidden[...] = hidden
    r.d_in[...] = d_in
    r.d_last[...] = d_last
    r.d_outlet[...] = d_outlet

    w1 = matrix(r, layer, "edge_first")
    w2 = matrix(r, layer, "edge_second")
    gain = vector(r, layer, "edge_gain")
    d_bias, d_offset, d_gain = (jnp.zeros((1, D), F32) for _ in range(3))
    to_send, to_recv = jnp.zeros((512, 256), F32), jnp.zeros((256, 256), F32)
    none = jnp.zeros((CHUNK, D), BF)
    for start in range(0, 2048, CHUNK):
        rows = slice(start, start + CHUNK)
        upper = r.upper[rows, :] > 0.5
        outside = r.outside[rows, :] > BF(0.5)
        upper_half = r.upper_half[rows, :] > BF(0.5)
        picked = dot(r.hot_recv[rows, :], r.own2[...])
        d_message = jnp.where(upper, picked[:, 128:], picked[:, :128])
        if has_edge_grad:
            d_message = d_message + r.edge_grad[rows, :]
        live = d_message * r.alive[rows, :]
        normal = r.normal[rows, :]
        d_gain = d_gain + jnp.sum(live * normal, axis=0, keepdims=True)
        d_second = layer_norm_back(live * gain, normal, r.inverse[rows, :])
        d_offset = d_offset + jnp.sum(d_second, axis=0, keepdims=True)
        d_second = d_second.astype(BF)
        d_act = dot_nt(d_second, w2).astype(BF).astype(F32)
        d_first = d_act * r.slope[rows, :]
        d_bias = d_bias + jnp.sum(d_first, axis=0, keepdims=True)
        d_half = d_first.astype(BF)
        r.d_second[rows, :] = d_second
        r.d_first[rows, :] = d_half
        split = jnp.concatenate([jnp.where(outside, none, d_half), jnp.where(outside, d_half, none)], axis=1)
        to_send = to_send + dot(r.hot_send_t[:, rows], split)
        split = jnp.concatenate([jnp.where(upper_half, none, d_half), jnp.where(upper_half, d_half, none)], axis=1)
        to_recv = to_recv + dot(r.hot_half_t[:, rows], split)
    r.vec[0:1, :] = d_bias
    r.vec[1:2, :] = d_offset
    r.vec[2:3, :] = d_gain
    r.vec[6:8, :] = jnp.zeros((2, D), F32)
    from_own = to_send[:, 0:128].astype(BF)
    from_halo = to_send[0:384, 128:256].astype(BF)
    at_recv = jnp.concatenate([to_recv[:, 0:128], to_recv[:, 128:256]], axis=0).astype(BF)
    d_halo = dot_nt(from_halo, w1[128:256]).astype(BF)
    r.sent0[...] = d_halo[0:128]
    r.sent1[...] = d_halo[0:128]
    r.sent2[...] = d_halo[128:256]
    r.sent3[...] = d_halo[256:384]
    r.grad_out[...] = grad + d_node_in[:, 0:128] + dot_nt(from_own, w1[128:256]) + dot_nt(at_recv, w1[256:384])
    r.from_own[...] = from_own
    r.from_halo[...] = from_halo
    r.at_recv[...] = at_recv


def late(r, layer, target, has_edge_grad, keep_edge_grad):
    def put(start, value):
        count = value.shape[0] // 8
        target[start : start + count, 0:8, :] = value.reshape(count, 8, D).astype(BF)

    own = r.latent[...].astype(BF)
    from_own, d_in = r.from_own[...], r.d_in[...]
    put(0, dot_tn(r.edge[...].astype(BF), r.d_first[...]))
    put(16, dot_tn(own, from_own) + dot_tn(r.halo[...], r.from_halo[...]))
    put(32, dot_tn(own, r.at_recv[...]))
    put(48, dot_tn(r.act[...], r.d_second[...]))
    put(64, dot_tn(jnp.concatenate([own, r.half[...]], axis=1), d_in))
    put(96, dot_tn(r.hidden[...], r.d_last[...]))
    put(112, dot_tn(r.half[...], r.d_outlet[...]))
    if keep_edge_grad:
        d_edge = dot_nt(r.d_first[...], matrix(r, layer, "edge_first")[0:128]).astype(BF).astype(F32)
        r.edge_grad_out[...] = d_edge + r.edge_grad[...] if has_edge_grad else d_edge


def pack(r):
    for layer, block in ((1, r.weights1), (2, r.weights2)):
        r.packed[:, 8 * layer : 8 * layer + 8, :] = block[...]
    vec = jnp.concatenate([r.vec[...], r.vec1[...], r.vec2[...]], axis=0)
    top = vec.astype(BF).astype(F32)
    rest = (vec - top).astype(BF).astype(F32)
    turned = jnp.transpose(jnp.concatenate([top, rest, jnp.zeros((80, D), F32)], axis=0))
    turned = jnp.broadcast_to(turned.reshape(128, 1, D), (128, 8, D))
    r.packed[:, 24:32, :] = jnp.where(lax.broadcasted_iota(I32, turned.shape, 1) == 0, turned, 0.0).astype(BF)
    r.given[...] = r.packed[pl.ds(64 * (1 - lax.axis_index("core")), 64)]


def two_terms(block):
    axis = block.ndim - 2
    value = jnp.sum(block, axis=axis, keepdims=True)
    top = value.astype(BF).astype(F32)
    line = lax.broadcasted_iota(I32, block.shape, axis)
    return jnp.where(line == 0, top, jnp.where(line == 1, value - top, 0.0)).astype(BF)


def pair_sum(r):
    total = r.packed[pl.ds(64 * lax.axis_index("core"), 64)].astype(F32) + r.got[...].astype(F32)
    r.chip[:, 0:24, :] = total[:, 0:24].astype(BF)
    r.chip[:, 24:32, :] = two_terms(total[:, 24:32])


def middle(r):
    r.latent_grad[...] = r.top_grad[...] + returned_sum(r)
    total = jnp.sum(r.shares[...].astype(F32), axis=0)
    r.summed[0:24, :] = total[0:24].astype(BF)
    r.summed[24:32, :] = two_terms(total[24:32])


def finish(r):
    core = lax.axis_index("core")
    r.whole[pl.ds(64 * core, 64)] = r.mine[...]
    r.whole[pl.ds(64 * (1 - core), 64)] = r.other[...]
    for layer in range(3):
        for name, (first, count) in PLACES.items():
            block = r.whole[first // 8 : (first + count) // 8, 8 * layer : 8 * layer + 8, :]
            getattr(r, name)[layer] = block.astype(F32).reshape(count, D)
    turned = jnp.transpose(jnp.sum(r.whole[:, 24:32, :].astype(F32), axis=1))
    vec = turned[0:24] + turned[24:48]
    for layer in range(3):
        for name, k in LINES.items():
            getattr(r, name)[layer : layer + 1, :] = vec[8 * layer + k : 8 * layer + k + 1, :]


SENT = dict(sent0=((128, D), BF), sent1=((128, D), BF), sent2=((128, D), BF), sent3=((128, D), BF))
LOADED = dict(
    edge=((2048, D), BF),
    top_grad=((512, D), F32),
    weights=((3, 1024, D), BF),
    vectors=((3, 8, D), F32),
    hot_send=((2048, 512), BF),
    hot_recv=((2048, 256), BF),
    places=((16, D), I32),
    hot_half_t=((256, 2048), BF),
    outside=((2048, D), BF),
    upper=((2048, D), F32),
    upper_half=((2048, D), BF),
    alive=((2048, D), F32),
    flag=((512, D), F32),
)
FORWARD_SCRATCH = dict(ext2=((512, 256), BF))
PAIR_SCRATCH = dict(own2=((256, 256), BF))
RESIDUALS = dict(
    act=((2048, D), BF),
    slope=((2048, D), F32),
    normal=((2048, D), F32),
    inverse=((2048, D), F32),
    zn=((512, D), F32),
    pn=((512, D), F32),
    half=((512, D), BF),
    halo=((384, D), BF),
)
HANDED = dict(
    hidden=((512, D), BF),
    d_in=((512, D), BF),
    d_last=((512, D), BF),
    d_outlet=((512, D), BF),
    d_second=((2048, D), BF),
    d_first=((2048, D), BF),
    from_own=((512, D), BF),
    from_halo=((384, D), BF),
    at_recv=((512, D), BF),
)


def pairs(count, odd):
    steps = []
    for low in range(odd, count - 1, 2):
        steps += [(low, low + 1), (low + 1, low)]
    return steps


def exchange(made):
    sub = lax.axis_size("x") * lax.axis_size("core")
    dom = lax.axis_size("dom")
    far = lax.ppermute(made["sent1"], SUB, pairs(sub, 1))
    near = lax.ppermute(made["sent0"], SUB, pairs(sub, 0))
    return (
        near,
        far,
        lax.ppermute(made["sent2"], "dom", pairs(dom, 0)),
        lax.ppermute(made["sent3"], "dom", pairs(dom, 1)),
    )


def halo_of(made):
    h0, h1, h2, h3 = exchange(made)
    return dict(halo2=h2, halo3=h3, halo1=h1, halo0=h0)


def back_of(made):
    b0, b1, b2, b3 = exchange(made)
    return dict(back2=b2, back3=b3, back1=b1, back0=b0)


def on_device(
    nodes,
    edges,
    senders,
    receivers,
    edge_live,
    outlet_flags,
    send_rows,
    edge_first,
    edge_bias,
    edge_second,
    edge_offset,
    edge_gain,
    node_first,
    node_bias,
    node_second,
    node_offset,
    node_gain,
    outlet_map,
    grad_out,
):
    params = dict(
        edge_first=edge_first,
        edge_bias=edge_bias,
        edge_second=edge_second,
        edge_offset=edge_offset,
        edge_gain=edge_gain,
        node_first=node_first,
        node_bias=node_bias,
        node_second=node_second,
        node_offset=node_offset,
        node_gain=node_gain,
        outlet_map=outlet_map,
    )
    made = run(
        start_body,
        dict(nodes_in=nodes, rows_in=send_rows.reshape(3, D)),
        dict(SENT, picks=((384, 512), BF), spread=((512, 384), BF)),
        dict(nodes=((512, D), BF), rows=((3, D), I32), sem=((2,), None)),
        held=True,
    )
    picks, spread = dict(picks=made["picks"]), dict(spread=made["spread"])
    raw = dict(
        edge_in=edges,
        senders_in=senders.reshape(16, D),
        receivers_in=receivers.reshape(16, D),
        live_in=edge_live.reshape(16, D),
        flags_in=outlet_flags.reshape(4, D),
        top_grad_in=grad_out,
        **params,
    )
    index = ((16, D), I32)
    table = run(
        load_body,
        raw,
        LOADED,
        dict(
            senders=index,
            receivers=index,
            live=index,
            flags=((4, D), I32),
            sem=((len(raw),), None),
            **{name + "_raw": (value.shape, F32) for name, value in params.items()},
        ),
        flops=4 << 30,
        held=True,
    )
    edge, top_grad, places = table.pop("edge"), table.pop("top_grad"), table.pop("places")
    forward_table = dict(table)
    latent = nodes
    entered = []
    part = {}

    def begin(layer, latent, edge):
        ins = {name: table[name] for name in dict(weights=0, vectors=0, hot_recv=0, upper_half=0)}
        return run(
            lambda r: early(r, layer),
            dict(ins, latent=latent, edge=edge),
            dict(part=((2048, D), F32)),
            PAIR_SCRATCH,
            flops=2 << 30,
        )

    for layer in range(2):
        entry = dict(latent=latent, edge=edge)

        def forward(r, layer=layer):
            forward_part(r, layer, True, True, layer > 0)

        made = run(
            forward,
            dict(picks, **forward_table, **entry, **halo_of(made), **part),
            dict(SENT, latent_out=((512, D), F32), edge_out=((2048, D), F32), **RESIDUALS),
            dict(FORWARD_SCRATCH, **PAIR_SCRATCH),
            flops=4 << 30,
        )
        entered.append(dict(entry, **{name: made[name] for name in RESIDUALS}))
        latent, edge = made["latent_out"], made["edge_out"]
        part = begin(layer + 1, latent, edge)
        if layer == 0:
            late_table = run(
                place_body,
                dict(places=places, after=made["sent0"]),
                dict(hot_send_t=((512, 2048), BF)),
                flops=2 << 30,
            )
    table.update(late_table)
    backward_table = {name: table[name] for name in table if name not in dict(hot_send=0)}

    def turn(r):
        forward_part(r, 2, False, False, True)
        backward_part(r, 2, r.top_grad[...], False)

    gradient = dict(SENT, grad_out=((512, D), F32), vec=((8, D), F32))
    share = dict(weights_out=((128, 8, D), BF), edge_grad_out=((2048, D), F32))
    late_uses = dict(act=0, half=0, halo=0)
    made = run(
        turn,
        dict(table, **halo_of(made), latent=latent, edge=edge, top_grad=top_grad, **part),
        dict(
            gradient,
            latent_out=((512, D), F32),
            **HANDED,
            **{name: RESIDUALS[name] for name in late_uses},
        ),
        dict(
            FORWARD_SCRATCH,
            **PAIR_SCRATCH,
            **{name: RESIDUALS[name] for name in RESIDUALS if name not in late_uses},
        ),
        flops=12 << 30,
    )
    latent_out = made["latent_out"]
    late_ins = dict(weights=table["weights"])
    two = run(
        lambda r: late(r, 2, r.weights_out, False, True),
        dict(late_ins, latent=latent, edge=edge, **{name: made[name] for name in [*HANDED, *late_uses]}),
        share,
        flops=4 << 30,
    )
    done = dict(weights2=two["weights_out"], vec2=made["vec"])

    def backward_one(r):
        backward_part(r, 1, r.top_grad[...] + returned_sum(r), True)

    made = run(
        backward_one,
        dict(
            spread,
            **backward_table,
            **entered[1],
            **back_of(made),
            top_grad=made["grad_out"],
            edge_grad=two["edge_grad_out"],
        ),
        dict(gradient, **HANDED),
        PAIR_SCRATCH,
        flops=8 << 30,
    )
    one = run(
        lambda r: late(r, 1, r.weights_out, True, True),
        dict(
            late_ins,
            edge_grad=two["edge_grad_out"],
            **{name: made[name] for name in HANDED},
            **{name: entered[1][name] for name in dict(late_uses, latent=0, edge=0)},
        ),
        share,
        flops=4 << 30,
    )
    done.update(weights1=one["weights_out"], vec1=made["vec"])

    def backward_zero(r):
        backward_part(r, 0, r.top_grad[...] + returned_sum(r), True)
        late(r, 0, r.packed, True, False)
        pack(r)

    made = run(
        backward_zero,
        dict(
            spread,
            **backward_table,
            **entered[0],
            **back_of(made),
            top_grad=made["grad_out"],
            edge_grad=one["edge_grad_out"],
            **done,
        ),
        dict(gradient, packed=((128, 32, D), BF), given=((64, 32, D), BF)),
        dict(PAIR_SCRATCH, **HANDED),
        flops=8 << 30,
    )
    swap = [(0, 1), (1, 0)]
    got = lax.ppermute(made["given"], "core", swap)
    chip = run(pair_sum, dict(packed=made["packed"], got=got), dict(chip=((64, 32, D), BF)))["chip"]
    shares = lax.all_to_all(chip, PEERS, 0, 0, tiled=True)
    mid = run(
        middle,
        dict(spread, top_grad=made["grad_out"], shares=shares, **back_of(made)),
        dict(latent_grad=((512, D), F32), summed=((32, D), BF)),
    )
    spread = jnp.broadcast_to(mid["summed"][None], (64, 32, D))
    mine = lax.all_to_all(spread, PEERS, 0, 0, tiled=True)
    other = lax.ppermute(mine, "core", swap)
    results = run(
        finish,
        dict(mine=mine, other=other),
        {name: (value.shape, F32) for name, value in params.items()},
        dict(whole=((128, 32, D), BF)),
    )
    return (latent_out, mid["latent_grad"]) + tuple(results[name] for name in params)


def solution(mesh):
    inner = Mesh(mesh.devices.reshape(mesh.devices.shape[0], -1, 2), AXES)
    split = P(AXES, None)
    flat = P(AXES)
    placed = (split, split) + (flat,) * 5 + (P(),) * 11 + (split,)
    return jax.shard_map(
        on_device,
        mesh=inner,
        in_specs=placed,
        out_specs=(split, split) + (P(),) * 11,
        check_vma=False,
    )
```
